32 devices in a mesh: pipe: 2 (over core), node: 8 (over z, x), head: 2 (over y).
Axes of the slice: x: 2, y: 2, z: 4, core: 2. Of those that a mesh axis runs over, the one named last changes fastest.
Arguments:
- feats: bfloat16 [2, 1024, 2048], P(None, 'node', 'head'), may hold values from -20 to 20
- gain: float32 [2, 2048], P('pipe'), may hold values from 0.25 to 1.75
- w_qkv: bfloat16 [2, 3, 2048, 2048], P('pipe', None, 'node', 'head'), may hold values from -0.176776695 to 0.176776695
- w_out: bfloat16 [2, 2048, 2048], P('pipe', 'head', 'node'), may hold values from -1 to 1
- block_mask: int32 [2, 8, 8], replicated, may hold values from 0 to 1, as said below
Outputs:
- layers_out: bfloat16 [2, 2, 1024, 2048], P('pipe', None, 'node', 'head')
The draws below stay inside these ranges and needn't reach their ends.
Inputs may be any that keep to these rules, and one draw needn't show every extreme that they name: block_mask[m, b, b] = 1; block_mask[m, b, c] is 0 unless c = b or c = b xor 2^k with k one of L - 1, L // 2 and 0, where 2^L = 8.
All inputs are finite; a program needn't handle non-finite values.
Results may differ from the reference program's by a relative error of at most 0.023.
Values may be sent and summed in bfloat16 or wider, within the bound.
A program may use at most 64 MiB of HBM per device.

```python
import math
import jax
import jax.numpy as jnp
from jax import lax

D = 2048
HEADS = 16
HD = 128
BLOCK = 128
MICRO = 2
NBLK = 8
NODES = 1024
SEGMENTS = 2


def shared_signs(key):
    picks = jax.random.randint(jax.random.fold_in(key, 101), (D,), 0, 2)
    return picks.astype(jnp.float32) * 2.0 - 1.0


def draw_feats(key, part):
    signs = shared_signs(key)
    chosen = max(2, BLOCK // 32)
    spacing = BLOCK // chosen
    offset = jax.random.randint(jax.random.fold_in(key, 202), (MICRO, NBLK, 1), 0, spacing)
    places = jnp.arange(BLOCK, dtype=jnp.int32)[None, None, :]
    picked = (places - offset) % spacing == 0
    strength = jnp.exp(jax.random.uniform(jax.random.fold_in(key, 303), (MICRO, NBLK, BLOCK), jnp.float32, math.log(3.0), math.log(14.0)))
    lifted = jnp.where(picked, strength, 0.0).reshape(MICRO, NODES, 1)
    noise = jax.random.truncated_normal(jax.random.fold_in(key, 404), -6.0, 6.0, (MICRO, NODES, D), jnp.float32)
    return (lifted * signs[None, None, :] + noise).astype(jnp.bfloat16)


def draw_w_qkv(key, part):
    unit_dir = shared_signs(key) * D ** (-0.5)
    spread = D ** (-0.5)
    base = jax.random.truncated_normal(jax.random.fold_in(key, 505), -6.0, 6.0, (SEGMENTS, 3, D, D), jnp.float32) * spread
    column_bits = jax.random.randint(jax.random.fold_in(key, 606), (SEGMENTS, D), 0, 2)
    column_signs = column_bits.astype(jnp.float32) * 2.0 - 1.0
    head_strength = jnp.exp(jax.random.uniform(jax.random.fold_in(key, 707), (SEGMENTS, HEADS), jnp.float32, math.log(1.2), math.log(2.4)))
    amplitude = jnp.sqrt(head_strength * (180.0 * HD ** 0.5 / D))
    columns = column_signs * jnp.repeat(amplitude, HD, axis=1) * HD ** (-0.5)
    lifted = unit_dir[None, :, None] * columns[:, None, :]
    select = jnp.array([1.0, 1.0, 0.0], dtype=jnp.float32)
    return (base + select[None, :, None, None] * lifted[:, None, :, :]).astype(jnp.bfloat16)


def draw_block_mask(key, part):
    rows = jnp.arange(NBLK, dtype=jnp.int32)[:, None]
    cols = jnp.arange(NBLK, dtype=jnp.int32)[None, :]
    width = NBLK.bit_length() - 1
    near = jnp.zeros((NBLK, NBLK), dtype=bool)
    for bit in [width - 1, width // 2, 0]:
        near = near | (jnp.bitwise_xor(rows, 1 << bit) == cols)
    coin = jax.random.randint(key, (MICRO, NBLK, NBLK), 0, 4) > 0
    ones = jnp.where(rows == cols, True, near[None] & coin)
    return jnp.where(ones, 1, 0).astype(jnp.int32)


def steps_of(key, shape, cuts, smallest, top_value):
    level, own = 1.0, jax.random.fold_in(key, 6)
    for position, parts in cuts:
        steps = jnp.exp(jax.random.uniform(jax.random.fold_in(own, position), (parts,), jnp.float32, smallest / len(cuts), top_value / len(cuts)))
        level = level * jnp.repeat(steps, shape[position] // parts).reshape([-1 if axis == position else 1 for axis in range(len(shape))])
    return level


def normal_values(own_key, shape, deviation, limit, cuts=(), kind=jnp.bfloat16):
    entries = deviation * jax.random.normal(own_key, shape, jnp.float32)
    if cuts:
        entries = entries * steps_of(own_key, shape, cuts, -0.22, 0.18)
    return jnp.clip(entries, -limit, limit).astype(kind)


def setup_inputs(seed: int = 0) -> dict:
    seeds = jax.random.split(jax.random.key(seed), 6)
    return {
        "feats": draw_feats(jax.random.fold_in(seeds[5], 71), 0),
        "gain": jnp.clip(1.0 + 0.15 * jax.random.normal(seeds[1], (SEGMENTS, D), jnp.float32), 0.25, 1.75),
        "w_qkv": draw_w_qkv(jax.random.fold_in(seeds[5], 71), 0),
        "w_out": normal_values(seeds[3], (SEGMENTS, D, D), (D // 64) ** -0.5, 1.0, ((0, 2), (1, 2), (2, 8))),
        "block_mask": draw_block_mask(jax.random.fold_in(seeds[5], 71), 0),
    }


EPS = 1e-06
NEG = -1e+30

def partner_bits():
    width = NBLK.bit_length() - 1
    return [width - 1, width // 2, 0]

def layer(x, gain_row, w_qkv_s, w_out_s, mask_m):
    xf = x.astype(jnp.float32)
    inv = lax.rsqrt(lax.optimization_barrier(jnp.mean(xf * xf, axis=-1, keepdims=True)) + EPS)
    normed = (xf * inv * gain_row).astype(jnp.bfloat16)
    query = jnp.dot(normed, w_qkv_s[0], preferred_element_type=jnp.float32).astype(jnp.bfloat16)
    key = jnp.dot(normed, w_qkv_s[1], preferred_element_type=jnp.float32).astype(jnp.bfloat16)
    value = jnp.dot(normed, w_qkv_s[2], preferred_element_type=jnp.float32).astype(jnp.bfloat16)
    q_blocks = query.reshape(NBLK, BLOCK, HEADS, HD)
    k_blocks = key.reshape(NBLK, BLOCK, HEADS, HD)
    v_blocks = value.reshape(NBLK, BLOCK, HEADS, HD)
    scale = 1.0 / HD ** 0.5

    def one_block(index):
        idx = [index] + [jnp.bitwise_xor(index, 1 << bit) for bit in partner_bits()]
        idx = jnp.stack(idx).astype(jnp.int32)
        flags = mask_m[index, idx] > 0
        keep = jnp.repeat(flags, BLOCK)
        kb = k_blocks[idx].reshape(len(partner_bits()) * BLOCK + BLOCK, HEADS, HD)
        vb = v_blocks[idx].reshape(len(partner_bits()) * BLOCK + BLOCK, HEADS, HD)
        qb = q_blocks[index]
        scores = jnp.einsum('qhd,khd->hqk', qb.astype(jnp.float32), kb.astype(jnp.float32)) * scale
        scores = jnp.where(keep[None, None, :], scores, NEG)
        top = lax.optimization_barrier(jnp.max(scores, axis=-1, keepdims=True))
        expo = jnp.where(keep[None, None, :], jnp.exp(scores - top), 0.0)
        total = lax.optimization_barrier(jnp.sum(expo, axis=-1))
        weights = expo.astype(jnp.bfloat16)
        summed = jnp.einsum('hqk,khd->hqd', weights.astype(jnp.float32), vb.astype(jnp.float32))
        out = summed / total[..., None]
        return jnp.transpose(out, (1, 0, 2)).reshape(BLOCK, D).astype(jnp.bfloat16)
    attended = lax.map(one_block, jnp.arange(NBLK, dtype=jnp.int32)).reshape(NODES, D)
    projected = jnp.dot(attended, w_out_s, preferred_element_type=jnp.float32)
    return (xf + projected).astype(jnp.bfloat16)

def reference(feats, gain, w_qkv, w_out, block_mask):
    first = []
    second = []
    for micro in range(MICRO):
        mid = layer(feats[micro], gain[0], w_qkv[0], w_out[0], block_mask[micro])
        first.append(mid)
        second.append(layer(mid, gain[1], w_qkv[1], w_out[1], block_mask[micro]))
    return jnp.stack([jnp.stack(first), jnp.stack(second)])
```

```python
import functools
import jax
import jax.numpy as jnp
from jax import lax
from jax.experimental import pallas as pl
from jax.experimental.pallas import tpu as pltpu
from jax.sharding import PartitionSpec as P

HD = 128
MICRO = 2


EPS = 1e-06
NEG = -1e30


def from_partner(block, axis, apart):
    count = lax.axis_size(axis)
    route = []
    for low in range(count):
        high = low | 1 << apart
        if high != low and high < count:
            route += [(low, high), (high, low)]
    return lax.ppermute(block, axis, route)


def from_behind(value, axis, steps):
    count = lax.axis_size(axis)
    first, last = (max(0, -steps), min(count, count - steps))
    return lax.ppermute(value, axis, [(source, source + steps) for source in range(first, last)])


def partial_attend(query, key, value, keep):
    rows = query.shape[0]
    groups = query.shape[1] // HD
    q_heads = query.reshape(rows, groups, HD)
    k_heads = key.reshape(key.shape[0], groups, HD)
    v_heads = value.reshape(value.shape[0], groups, HD)
    scores = jnp.einsum("qhd,khd->hqk", q_heads, k_heads, preferred_element_type=jnp.float32) * (
        1.0 / HD**0.5
    )
    scores = jnp.where(keep[None, None, :], scores, NEG)
    top = jnp.max(scores, axis=-1)
    expo = jnp.where(keep[None, None, :], jnp.exp(scores - top[..., None]), 0.0)
    total = jnp.sum(expo, axis=-1)
    summed = jnp.einsum(
        "hqk,khd->hqd", expo.astype(jnp.bfloat16), v_heads, preferred_element_type=jnp.float32
    )
    return (summed, top, total)


def finish(summed, total):
    out = summed / total[..., None]
    rows = out.shape[1]
    return jnp.transpose(out, (1, 0, 2)).reshape(rows, -1).astype(jnp.bfloat16)


def local_any(feats, gain, w_qkv, w_out, block_mask):
    segment = lax.axis_index("pipe")
    me = lax.axis_index("node")
    width = lax.axis_size("node").bit_length() - 1
    bit_list = [width - 1, width // 2, 0]
    qkv_whole, out_whole = (
        lax.all_gather(w_qkv, "node", axis=2, tiled=True),
        lax.all_gather(w_out, "node", axis=2, tiled=True),
    )
    w_query = qkv_whole[0, 0]
    w_key = qkv_whole[0, 1]
    w_value = qkv_whole[0, 2]
    w_proj = out_whole[0]
    gain_row = gain[0]
    rows = feats.shape[1]
    carried = jnp.zeros_like(feats[0])
    results = []
    for tick in range(MICRO + 1):
        micro = jnp.clip(tick - segment, 0, MICRO - 1)
        fresh = feats[min(tick, MICRO - 1)]
        inputs = jnp.where(segment == 0, fresh, carried)
        whole = lax.all_gather(inputs, "head", axis=1, tiled=True)
        xf = whole.astype(jnp.float32)
        inv = lax.rsqrt(jnp.mean(xf * xf, axis=-1, keepdims=True) + EPS)
        normed = (xf * inv * gain_row).astype(jnp.bfloat16)
        query = jnp.dot(normed, w_query, preferred_element_type=jnp.float32).astype(jnp.bfloat16)
        key = jnp.dot(normed, w_key, preferred_element_type=jnp.float32).astype(jnp.bfloat16)
        value = jnp.dot(normed, w_value, preferred_element_type=jnp.float32).astype(jnp.bfloat16)
        mask_rows = lax.dynamic_index_in_dim(block_mask, micro, 0, keepdims=False)
        own_flag = mask_rows[me, me] > 0
        key_list = [key]
        value_list = [value]
        flag_list = [own_flag]
        for bit in bit_list:
            far_key, far_value = from_partner((key, value), "node", bit)
            key_list.append(far_key)
            value_list.append(far_value)
            flag_list.append(mask_rows[me, jnp.bitwise_xor(me, 1 << bit)] > 0)
        keep = jnp.repeat(jnp.stack(flag_list), rows)
        summed, top, total = partial_attend(
            query, jnp.concatenate(key_list, 0), jnp.concatenate(value_list, 0), keep
        )
        attended = finish(summed, total)
        terms = jnp.dot(attended, w_proj, preferred_element_type=jnp.float32)
        reduced = lax.psum_scatter(
            terms.astype(jnp.bfloat16), "head", scatter_dimension=1, tiled=True
        ).astype(jnp.float32)
        output = (inputs.astype(jnp.float32) + reduced).astype(jnp.bfloat16)
        results.append(output)
        if tick < MICRO:
            carried = from_behind(output, "pipe", 1)
    first = jnp.where(segment == 0, results[0], results[1])
    second = jnp.where(segment == 0, results[1], results[2])
    return jnp.stack([first, second])[None]


MESH_ID = pl.DeviceIdType.MESH
ANY = pl.BlockSpec(memory_space=pl.ANY)


def place():
    core, node, y = lax.axis_index("pipe"), lax.axis_index("node"), lax.axis_index("head")
    return core, lax.rem(node, 2), y, lax.div(node, 2)


def dev(core, x, y, z):
    return (core, z * 2 + x, y)


def z_apart(z, d):
    if d == 0:
        return z
    if d == 1:
        return z + 1 - 2 * lax.rem(z, 2)
    if d == 2:
        return z + 2 - 4 * lax.div(z, 2)
    return 3 - z


def remote(src, dst, send, recv, target):
    return pltpu.make_async_remote_copy(
        src_ref=src, dst_ref=dst, send_sem=send, recv_sem=recv, device_id=target, device_id_type=MESH_ID
    )


def greet(peers):
    barrier = pltpu.get_barrier_semaphore()
    for peer in peers:
        pl.semaphore_signal(barrier, inc=1, device_id=peer, device_id_type=MESH_ID)
    pl.semaphore_wait(barrier, len(peers))


def head_slot(core, y, z):
    return 8 * y + 2 * z + core


def column_slot(core, y, z):
    return 4 * z + 2 * y + core


def columns_kernel(slot, own, out, local_sem, z_send, z_recv, y_send, y_recv, b_send, b_recv):
    core, x, y, z = place()
    wide = own.shape[1]

    def region(c, yy, zz):
        return out.at[:, pl.ds(pl.multiple_of(slot(c, yy, zz) * wide, wide), wide)]

    far = [dev(core, x, y, z_apart(z, d)) for d in (1, 2, 3)]
    beside, sibling = dev(core, x, 1 - y, z), dev(1 - core, x, y, z)
    greet(far + [beside, sibling])
    sent = []

    def send(src, dst, ssem, rsem, target):
        copy = remote(src, dst, ssem, rsem, target)
        copy.start()
        sent.append(copy)

    mine = region(core, y, z)
    send(own, mine, y_send.at[0], y_recv.at[0], beside)
    for d in (3, 2, 1):
        send(own, mine, z_send.at[d - 1], z_recv.at[d - 1], far[d - 1])
    send(own, mine, b_send.at[0], b_recv.at[0], sibling)
    keep = pltpu.make_async_copy(own, mine, local_sem)
    keep.start()
    for d in (1, 2, 3):
        got = region(core, y, z_apart(z, d))
        remote(own, got, z_send.at[d - 1], z_recv.at[d - 1], sibling).wait_recv()
        send(got, got, y_send.at[d], y_recv.at[d], beside)
        send(got, got, b_send.at[d], b_recv.at[d], sibling)
    for d in range(4):
        got = region(core, 1 - y, z_apart(z, d))
        remote(own, got, y_send.at[d], y_recv.at[d], sibling).wait_recv()
        send(got, got, b_send.at[4 + d], b_recv.at[4 + d], sibling)
    for d in range(8):
        got = region(1 - core, y if d < 4 else 1 - y, z_apart(z, d % 4))
        remote(own, got, b_send.at[d], b_recv.at[d], sibling).wait_recv()
    for copy in sent:
        copy.wait_send()
    keep.wait()


def all_columns(own, slot, ident):
    dma = pltpu.SemaphoreType.DMA
    return pl.pallas_call(
        functools.partial(columns_kernel, slot),
        out_shape=jax.ShapeDtypeStruct((own.shape[0], own.shape[1] * 16), own.dtype),
        in_specs=[ANY],
        out_specs=ANY,
        scratch_shapes=[dma(()), dma((3,)), dma((3,)), dma((4,)), dma((4,)), dma((8,)), dma((8,))],
        compiler_params=pltpu.CompilerParams(collective_id=ident, has_side_effects=True),
        name="all_columns_%d" % ident,
    )(own)


def spread_kernel(
    feats, gain, w_qkv, w_out, xg, gains, wq, wo,
    l_sem, x_send, x_recv, z_send, z_recv, y_send, y_recv, b_send, b_recv,
    g_send, g_recv, q_send, q_recv, qx_send, qx_recv, o_send, o_recv,
):
    core, x, y, z = place()
    node = z * 2 + x
    half, wide = feats.shape[1] // 2, feats.shape[2]
    depth = w_qkv.shape[2]
    far = [z_apart(z, d) for d in (1, 2, 3)]
    beside, sibling, across = dev(core, x, 1 - y, z), dev(1 - core, x, y, z), dev(core, 1 - x, y, z)
    plane = [
        dev(cc, xx, yy, z)
        for cc in (core, 1 - core)
        for xx in (x, 1 - x)
        for yy in (y, 1 - y)
    ][1:]
    greet(plane + [dev(cc, x, y, zz) for zz in far for cc in (core, 1 - core)])
    sent = []
    local = []

    def send(src, dst, ssem, rsem, target):
        copy = remote(src, dst, ssem, rsem, target)
        copy.start()
        sent.append(copy)

    def keep(src, dst, sem):
        copy = pltpu.make_async_copy(src, dst, sem)
        copy.start()
        local.append(copy)

    def region(c, xx, yy, zz):
        return xg.at[
            pl.ds(pl.multiple_of((zz * 2 + xx) * 2 * half + c * half, half), half),
            pl.ds(pl.multiple_of(yy * wide, wide), wide),
        ]

    rows = pl.ds(pl.multiple_of(core * half, half), half)
    mine, other = feats.at[x, rows, :], feats.at[1 - x, rows, :]
    spot = region(core, x, y, z)
    send(other, spot, x_send, x_recv, across)
    send(mine, spot, y_send.at[0], y_recv.at[0], beside)
    for d in (3, 2, 1):
        send(mine, spot, z_send.at[d - 1], z_recv.at[d - 1], dev(core, x, y, far[d - 1]))
    send(mine, spot, b_send.at[0], b_recv.at[0], sibling)
    keep(mine, spot, l_sem.at[0])
    send(gain, gains.at[core], g_send, g_recv, sibling)
    keep(gain, gains.at[core], l_sem.at[1])

    def head_columns(zz, c):
        return w_qkv.at[0, :, :, pl.ds(pl.multiple_of((zz * 2 + c) * HD, HD), HD)]

    def depth_rows(c, xx, zz):
        return wq.at[c, :, pl.ds(pl.multiple_of((zz * 2 + xx) * depth, depth), depth), :]

    own_rows = depth_rows(core, x, z)
    for d in (0, 3, 2, 1):
        zz = z_apart(z, d)
        for other_core in range(2):
            target = 1 - core if other_core else core
            if d == 0 and not other_core:
                keep(head_columns(z, core), own_rows, l_sem.at[2])
                send(head_columns(z, core), own_rows, qx_send.at[0], qx_recv.at[0], across)
            else:
                at = 2 * d + other_core
                send(head_columns(zz, target), own_rows, q_send.at[at], q_recv.at[at], dev(target, x, y, zz))

    half_rows = w_out.shape[1]
    to = wo.at[core, pl.ds(pl.multiple_of(y * half_rows, half_rows), half_rows), :]
    projections = []
    for a in range(2):
        for b in range(2):
            xx = 1 - x if a else x
            cc = 1 - core if b else core
            src = w_out.at[0, :, pl.ds(pl.multiple_of(cc * HD, HD), HD)]
            rsem = o_recv.at[2 * y + core]
            copy = remote(src, to, o_send.at[2 * a + b], rsem, dev(cc, xx, x, z))
            if a == 0 and b == 0:
                pl.when(x != y)(copy.start)
                pl.when(x == y)(pltpu.make_async_copy(src, to, rsem).start)
            else:
                copy.start()
            projections.append(copy)

    far_x = region(core, 1 - x, y, z)
    remote(mine, far_x, x_send, x_recv, sibling).wait_recv()
    send(far_x, far_x, y_send.at[4], y_recv.at[4], beside)
    for d in (3, 2, 1):
        send(far_x, far_x, z_send.at[2 + d], z_recv.at[2 + d], dev(core, x, y, far[d - 1]))
    send(far_x, far_x, b_send.at[8], b_recv.at[8], sibling)
    for k in range(2):
        xx = 1 - x if k else x
        for d in (1, 2, 3):
            got = region(core, xx, y, far[d - 1])
            remote(mine, got, x_send, z_recv.at[3 * k + d - 1], sibling).wait_recv()
            send(got, got, y_send.at[4 * k + d], y_recv.at[4 * k + d], beside)
            send(got, got, b_send.at[8 * k + d], b_recv.at[8 * k + d], sibling)
    for d in range(4):
        for other_core in range(2):
            at = 2 * d + other_core
            if at == 0:
                continue
            got = depth_rows(1 - core if other_core else core, x, z_apart(z, d))
            remote(head_columns(z, core), got, x_send, q_recv.at[at], sibling).wait_recv()
            send(got, got, qx_send.at[at], qx_recv.at[at], across)
    for k in range(2):
        xx = 1 - x if k else x
        for d in range(4):
            got = region(core, xx, 1 - y, z_apart(z, d))
            remote(mine, got, x_send, y_recv.at[4 * k + d], sibling).wait_recv()
            send(got, got, b_send.at[8 * k + 4 + d], b_recv.at[8 * k + 4 + d], sibling)
    for k in range(2):
        xx = 1 - x if k else x
        for d in range(8):
            got = region(1 - core, xx, y if d < 4 else 1 - y, z_apart(z, d % 4))
            remote(mine, got, x_send, b_recv.at[8 * k + d], sibling).wait_recv()
    for d in range(4):
        for other_core in range(2):
            at = 2 * d + other_core
            got = depth_rows(1 - core if other_core else core, 1 - x, z_apart(z, d))
            remote(head_columns(z, core), got, x_send, qx_recv.at[at], sibling).wait_recv()
    remote(gain, gains.at[1 - core], g_send, g_recv, sibling).wait_recv()
    for yy in range(2):
        for cc in range(2):
            got = wo.at[cc, pl.ds(yy * half_rows, half_rows), :]
            remote(w_out.at[0, :, pl.ds(0, HD)], got, x_send, o_recv.at[2 * yy + cc], sibling).wait_recv()
    for copy in sent:
        copy.wait_send()
    for copy in local:
        copy.wait()
    pl.when(x != y)(projections[0].wait_send)
    for copy in projections[1:]:
        copy.wait_send()


def spread(feats, gain, w_qkv, w_out):
    dma = pltpu.SemaphoreType.DMA
    bf = jnp.bfloat16
    rows, wide = feats.shape[1] * 8, feats.shape[2] * 2
    return pl.pallas_call(
        spread_kernel,
        out_shape=(
            jax.ShapeDtypeStruct((rows, wide), bf),
            jax.ShapeDtypeStruct((2, 1, wide), jnp.float32),
            jax.ShapeDtypeStruct((2, 3, wide, HD), bf),
            jax.ShapeDtypeStruct((2, wide, HD), bf),
        ),
        in_specs=[ANY] * 4,
        out_specs=(ANY,) * 4,
        scratch_shapes=[dma((3,)), dma(()), dma(()), dma((6,)), dma((6,)), dma((8,)), dma((8,)), dma((16,)), dma((16,)),
                        dma(()), dma(()), dma((8,)), dma((8,)), dma((8,)), dma((8,)), dma((4,)), dma((4,))],
        compiler_params=pltpu.CompilerParams(collective_id=0, has_side_effects=True),
        name="spread",
    )(feats, gain, w_qkv, w_out)


def deliver_kernel(mid, last, out, l_sem, m_send, m_recv, a_send, a_recv):
    core, x, y, z = place()
    node = z * 2 + x
    rows, wide = out.shape[1], out.shape[2]
    piece = last.shape[1]
    to_y = lax.div(z, 2)
    z_low = lax.rem(z, 2)
    first = core == 0
    to_self = (core == 1) & (y == to_y)
    barrier = pltpu.get_barrier_semaphore()

    def signal(peer):
        pl.semaphore_signal(barrier, inc=1, device_id=peer, device_id_type=MESH_ID)

    @pl.when(first)
    def _():
        signal(dev(0, 1 - x, y, z))

    sources = [(zl, xx, yy, cc) for zl in range(2) for xx in range(2) for yy in range(2) for cc in range(2)]
    for zl, xx, yy, cc in sources:
        own = (cc == core) & (xx == x) & (yy == y) & (2 * y + zl == z)

        @pl.when((core == 1) & jnp.logical_not(own))
        def _():
            signal(dev(cc, xx, yy, 2 * y + zl))

    pl.semaphore_wait(barrier, 8 - to_self.astype(jnp.int32) + first.astype(jnp.int32))

    def mid_rows(n):
        return mid.at[
            pl.ds(pl.multiple_of(n * rows, rows), rows), pl.ds(pl.multiple_of(y * wide, wide), wide)
        ]

    cross = remote(mid_rows(z * 2 + 1 - x), out.at[x], m_send, m_recv, dev(0, 1 - x, y, z))
    keep = pltpu.make_async_copy(mid_rows(node), out.at[x], l_sem)

    @pl.when(first)
    def _():
        cross.start()
        keep.start()

    slot = 4 * z_low + 2 * y + core
    spot = out.at[x, :, pl.ds(pl.multiple_of(slot * piece, piece), piece)]
    index = 8 * z_low + 4 * x + 2 * y + core
    copies = []
    for n in range(8):
        src = last.at[pl.ds(n * rows, rows), :]
        copy = remote(src, spot, a_send.at[n], a_recv.at[index], dev(1, n % 2, to_y, n // 2))
        own = to_self & (node == n)
        pl.when(jnp.logical_not(own))(copy.start)
        pl.when(own)(pltpu.make_async_copy(src, spot, a_recv.at[index]).start)
        copies.append((copy, own))

    @pl.when(first)
    def _():
        remote(mid_rows(node), out.at[1 - x], m_send, m_recv, dev(0, 1 - x, y, z)).wait_recv()
        cross.wait_send()
        keep.wait()

    @pl.when(core == 1)
    def _():
        for zl, xx, yy, cc in sources:
            at = 4 * zl + 2 * yy + cc
            got = out.at[xx, :, pl.ds(at * piece, piece)]
            remote(
                last.at[pl.ds(0, rows), :], got, a_send.at[0], a_recv.at[8 * zl + 4 * xx + 2 * yy + cc],
                dev(0, x, y, z),
            ).wait_recv()

    for copy, own in copies:
        pl.when(jnp.logical_not(own))(copy.wait_send)


def deliver(mid, last):
    dma = pltpu.SemaphoreType.DMA
    return pl.pallas_call(
        deliver_kernel,
        out_shape=jax.ShapeDtypeStruct((2, mid.shape[0] // 8, mid.shape[1] // 2), mid.dtype),
        in_specs=[ANY] * 2,
        out_specs=ANY,
        scratch_shapes=[dma(()), dma(()), dma(()), dma((8,)), dma((16,))],
        compiler_params=pltpu.CompilerParams(collective_id=3, has_side_effects=True),
        name="deliver",
    )(mid, last)


def attend_kernel(x_ref, gain_ref, w_ref, flags, out_ref, q_ref, k_ref, v_ref):
    count = flags.shape[0]
    rows = x_ref.shape[0] // count
    step = 2 * rows
    width = count.bit_length() - 1
    bits = [width - 1, width // 2, 0]

    def project(at, _):
        span = pl.ds(pl.multiple_of(at * step, step), step)
        xf = x_ref[span, :].astype(jnp.float32)
        inv = lax.rsqrt(jnp.mean(xf * xf, axis=-1, keepdims=True) + EPS)
        normed = (xf * inv * gain_ref[...]).astype(jnp.bfloat16)
        for part, ref in enumerate((q_ref, k_ref, v_ref)):
            ref[span, :] = jnp.dot(normed, w_ref[part], preferred_element_type=jnp.float32).astype(jnp.bfloat16)
        return 0

    lax.fori_loop(0, x_ref.shape[0] // step, project, 0)
    for block in range(count):
        seen = [block] + [block ^ (1 << bit) for bit in bits]
        span = slice(block * rows, (block + 1) * rows)
        query = q_ref[span, :]
        scores = []
        for other in seen:
            key = k_ref[other * rows : (other + 1) * rows, :]
            dots = lax.dot_general(query, key, (((1,), (1,)), ((), ())), preferred_element_type=jnp.float32)
            scores.append(jnp.where(flags[block, other] > 0, dots * (1.0 / HD**0.5), NEG))
        top = functools.reduce(jnp.maximum, [jnp.max(s, axis=-1, keepdims=True) for s in scores])
        total = jnp.zeros_like(top)
        summed = jnp.zeros((rows, HD), jnp.float32)
        for other, s in zip(seen, scores):
            expo = jnp.where(flags[block, other] > 0, jnp.exp(s - top), 0.0)
            total = total + jnp.sum(expo, axis=-1, keepdims=True)
            summed = summed + jnp.dot(
                expo.astype(jnp.bfloat16), v_ref[other * rows : (other + 1) * rows, :],
                preferred_element_type=jnp.float32,
            )
        out_ref[span, :] = (summed / total).astype(jnp.bfloat16)


def attend(x, gain_row, w, flags):
    vmem = pl.BlockSpec(memory_space=pltpu.VMEM)
    rows = x.shape[0]
    return pl.pallas_call(
        attend_kernel,
        out_shape=jax.ShapeDtypeStruct((rows, HD), jnp.bfloat16),
        in_specs=[vmem, vmem, vmem, pl.BlockSpec(memory_space=pltpu.SMEM)],
        out_specs=vmem,
        scratch_shapes=[pltpu.VMEM((rows, HD), jnp.bfloat16)] * 3,
        compiler_params=pltpu.CompilerParams(vmem_limit_bytes=40 * 2**20),
        name="attend",
    )(x, gain_row, w, flags)


def local_planes(feats, gain, w_qkv, w_out, block_mask):
    core, micro, y, z = place()
    flags = lax.dynamic_index_in_dim(block_mask, micro, 0, keepdims=False)
    whole, gains, wq, wo = spread(feats, gain, w_qkv, w_out)
    column = column_slot(core, y, z) * HD

    def layer(x, s):
        attended = all_columns(attend(x, gains[s], wq[s], flags), head_slot, 1)
        projected = jnp.dot(attended, wo[s], preferred_element_type=jnp.float32)
        residual = lax.dynamic_slice_in_dim(x, column, HD, axis=1)
        return (residual.astype(jnp.float32) + projected).astype(jnp.bfloat16)

    mid = all_columns(layer(whole, 0), column_slot, 2)
    return deliver(mid, layer(mid, 1))[None]


def solution(mesh):
    planes = (mesh.shape["pipe"], mesh.shape["node"], mesh.shape["head"]) == (2, 8, 2)
    return jax.shard_map(
        local_planes if planes else local_any,
        mesh=mesh,
        in_specs=(
            P(None, "node", "head"),
            P("pipe", None),
            P("pipe", None, "node", "head"),
            P("pipe", "head", "node"),
            P(),
        ),
        out_specs=P("pipe", None, "node", "head"),
        check_vma=False,
    )
```

```python
import functools
import jax
import jax.numpy as jnp
from jax import lax
from jax.experimental import pallas as pl
from jax.experimental.pallas import tpu as pltpu
from jax.sharding import PartitionSpec as P

HD = 128
MICRO = 2


EPS = 1e-06
NEG = -1e30


def from_partner(block, axis, apart):
    count = lax.axis_size(axis)
    route = []
    for low in range(count):
        high = low | 1 << apart
        if high != low and high < count:
            route += [(low, high), (high, low)]
    return lax.ppermute(block, axis, route)


def from_behind(value, axis, steps):
    count = lax.axis_size(axis)
    first, last = (max(0, -steps), min(count, count - steps))
    return lax.ppermute(value, axis, [(source, source + steps) for source in range(first, last)])


def partial_attend(query, key, value, keep):
    rows = query.shape[0]
    groups = query.shape[1] // HD
    q_heads = query.reshape(rows, groups, HD)
    k_heads = key.reshape(key.shape[0], groups, HD)
    v_heads = value.reshape(value.shape[0], groups, HD)
    scores = jnp.einsum("qhd,khd->hqk", q_heads, k_heads, preferred_element_type=jnp.float32) * (
        1.0 / HD**0.5
    )
    scores = jnp.where(keep[None, None, :], scores, NEG)
    top = jnp.max(scores, axis=-1)
    expo = jnp.where(keep[None, None, :], jnp.exp(scores - top[..., None]), 0.0)
    total = jnp.sum(expo, axis=-1)
    summed = jnp.einsum(
        "hqk,khd->hqd", expo.astype(jnp.bfloat16), v_heads, preferred_element_type=jnp.float32
    )
    return (summed, top, total)


def finish(summed, total):
    out = summed / total[..., None]
    rows = out.shape[1]
    return jnp.transpose(out, (1, 0, 2)).reshape(rows, -1).astype(jnp.bfloat16)


def local_any(feats, gain, w_qkv, w_out, block_mask):
    segment = lax.axis_index("pipe")
    me = lax.axis_index("node")
    width = lax.axis_size("node").bit_length() - 1
    bit_list = [width - 1, width // 2, 0]
    qkv_whole, out_whole = (
        lax.all_gather(w_qkv, "node", axis=2, tiled=True),
        lax.all_gather(w_out, "node", axis=2, tiled=True),
    )
    w_query = qkv_whole[0, 0]
    w_key = qkv_whole[0, 1]
    w_value = qkv_whole[0, 2]
    w_proj = out_whole[0]
    gain_row = gain[0]
    rows = feats.shape[1]
    carried = jnp.zeros_like(feats[0])
    results = []
    for tick in range(MICRO + 1):
        micro = jnp.clip(tick - segment, 0, MICRO - 1)
        fresh = feats[min(tick, MICRO - 1)]
        inputs = jnp.where(segment == 0, fresh, carried)
        whole = lax.all_gather(inputs, "head", axis=1, tiled=True)
        xf = whole.astype(jnp.float32)
        inv = lax.rsqrt(jnp.mean(xf * xf, axis=-1, keepdims=True) + EPS)
        normed = (xf * inv * gain_row).astype(jnp.bfloat16)
        query = jnp.dot(normed, w_query, preferred_element_type=jnp.float32).astype(jnp.bfloat16)
        key = jnp.dot(normed, w_key, preferred_element_type=jnp.float32).astype(jnp.bfloat16)
        value = jnp.dot(normed, w_value, preferred_element_type=jnp.float32).astype(jnp.bfloat16)
        mask_rows = lax.dynamic_index_in_dim(block_mask, micro, 0, keepdims=False)
        own_flag = mask_rows[me, me] > 0
        key_list = [key]
        value_list = [value]
        flag_list = [own_flag]
        for bit in bit_list:
            far_key, far_value = from_partner((key, value), "node", bit)
            key_list.append(far_key)
            value_list.append(far_value)
            flag_list.append(mask_rows[me, jnp.bitwise_xor(me, 1 << bit)] > 0)
        keep = jnp.repeat(jnp.stack(flag_list), rows)
        summed, top, total = partial_attend(
            query, jnp.concatenate(key_list, 0), jnp.concatenate(value_list, 0), keep
        )
        attended = finish(summed, total)
        terms = jnp.dot(attended, w_proj, preferred_element_type=jnp.float32)
        reduced = lax.psum_scatter(
            terms.astype(jnp.bfloat16), "head", scatter_dimension=1, tiled=True
        ).astype(jnp.float32)
        output = (inputs.astype(jnp.float32) + reduced).astype(jnp.bfloat16)
        results.append(output)
        if tick < MICRO:
            carried = from_behind(output, "pipe", 1)
    first = jnp.where(segment == 0, results[0], results[1])
    second = jnp.where(segment == 0, results[1], results[2])
    return jnp.stack([first, second])[None]


PIECES = 4
MESH_ID = pl.DeviceIdType.MESH
ANY = pl.BlockSpec(memory_space=pl.ANY)


def place():
    core, node, y = lax.axis_index("pipe"), lax.axis_index("node"), lax.axis_index("head")
    return core, lax.rem(node, 2), y, lax.div(node, 2)


def dev(core, x, y, z):
    return (core, z * 2 + x, y)


def z_apart(z, d):
    if d == 0:
        return z
    if d == 1:
        return z + 1 - 2 * lax.rem(z, 2)
    if d == 2:
        return z + 2 - 4 * lax.div(z, 2)
    return 3 - z


def remote(src, dst, send, recv, target):
    return pltpu.make_async_remote_copy(
        src_ref=src, dst_ref=dst, send_sem=send, recv_sem=recv, device_id=target, device_id_type=MESH_ID
    )


def greet(peers):
    barrier = pltpu.get_barrier_semaphore()
    for peer in peers:
        pl.semaphore_signal(barrier, inc=1, device_id=peer, device_id_type=MESH_ID)
    pl.semaphore_wait(barrier, len(peers))


def head_slot(core, y, z):
    return 8 * y + 2 * z + core


def column_slot(core, y, z):
    return 4 * z + 2 * y + core


def columns_kernel(slot, own, out, local_sem, z_send, z_recv, y_send, y_recv, b_send, b_recv):
    core, x, y, z = place()
    wide = own.shape[1]
    rows = own.shape[0] // PIECES

    def region(c, yy, zz, p):
        return out.at[pl.ds(p * rows, rows), pl.ds(pl.multiple_of(slot(c, yy, zz) * wide, wide), wide)]

    far = [dev(core, x, y, z_apart(z, d)) for d in (1, 2, 3)]
    beside, sibling = dev(core, x, 1 - y, z), dev(1 - core, x, y, z)
    greet(far + [beside, sibling])
    sent = []

    def send(src, dst, ssem, rsem, target):
        copy = remote(src, dst, ssem, rsem, target)
        copy.start()
        sent.append(copy)

    for p in range(PIECES):
        mine, spot = own.at[pl.ds(p * rows, rows), :], region(core, y, z, p)
        for d in (1, 2, 3):
            send(mine, spot, z_send.at[p, d - 1], z_recv.at[p, d - 1], far[d - 1])
        send(mine, spot, y_send.at[p, 0], y_recv.at[p, 0], beside)
        send(mine, spot, b_send.at[p, 0], b_recv.at[p, 0], sibling)
    keep = pltpu.make_async_copy(own, out.at[:, pl.ds(pl.multiple_of(slot(core, y, z) * wide, wide), wide)], local_sem)
    keep.start()
    like = own.at[pl.ds(0, rows), :]
    for p in range(PIECES):
        for d in (1, 2, 3):
            got = region(core, y, z_apart(z, d), p)
            remote(like, got, z_send.at[p, d - 1], z_recv.at[p, d - 1], sibling).wait_recv()
            send(got, got, y_send.at[p, d], y_recv.at[p, d], beside)
            send(got, got, b_send.at[p, d], b_recv.at[p, d], sibling)
    for p in range(PIECES):
        for d in range(4):
            got = region(core, 1 - y, z_apart(z, d), p)
            remote(like, got, y_send.at[p, d], y_recv.at[p, d], sibling).wait_recv()
            send(got, got, b_send.at[p, 4 + d], b_recv.at[p, 4 + d], sibling)
    for p in range(PIECES):
        for d in range(8):
            got = region(1 - core, y if d < 4 else 1 - y, z_apart(z, d % 4), p)
            remote(like, got, b_send.at[p, d], b_recv.at[p, d], sibling).wait_recv()
    for copy in sent:
        copy.wait_send()
    keep.wait()


def all_columns(own, slot, ident):
    dma = pltpu.SemaphoreType.DMA
    counts = [(PIECES, c) for c in (3, 3, 4, 4, 8, 8)]
    return pl.pallas_call(
        functools.partial(columns_kernel, slot),
        out_shape=jax.ShapeDtypeStruct((own.shape[0], own.shape[1] * 16), own.dtype),
        in_specs=[ANY],
        out_specs=ANY,
        scratch_shapes=[dma(())] + [dma(c) for c in counts],
        compiler_params=pltpu.CompilerParams(collective_id=ident, has_side_effects=True),
        name="all_columns_%d" % ident,
    )(own)


def spread_kernel(
    feats, gain, w_qkv, w_out, xg, gains, wq, wo,
    l_sem, x_send, x_recv, z_send, z_recv, y_send, y_recv, b_send, b_recv,
    g_send, g_recv, q_send, q_recv, qx_send, qx_recv, o_send, o_recv,
):
    core, x, y, z = place()
    node = z * 2 + x
    half, wide = feats.shape[1] // 2, feats.shape[2]
    depth = w_qkv.shape[2]
    far = [z_apart(z, d) for d in (1, 2, 3)]
    beside, sibling, across = dev(core, x, 1 - y, z), dev(1 - core, x, y, z), dev(core, 1 - x, y, z)
    plane = [
        dev(cc, xx, yy, z)
        for cc in (core, 1 - core)
        for xx in (x, 1 - x)
        for yy in (y, 1 - y)
    ][1:]
    greet(plane + [dev(cc, x, y, zz) for zz in far for cc in (core, 1 - core)])
    sent = []
    local = []

    def send(src, dst, ssem, rsem, target):
        copy = remote(src, dst, ssem, rsem, target)
        copy.start()
        sent.append(copy)

    def keep(src, dst, sem):
        copy = pltpu.make_async_copy(src, dst, sem)
        copy.start()
        local.append(copy)

    def region(c, xx, yy, zz):
        return xg.at[
            pl.ds(pl.multiple_of((zz * 2 + xx) * 2 * half + c * half, half), half),
            pl.ds(pl.multiple_of(yy * wide, wide), wide),
        ]

    rows = pl.ds(pl.multiple_of(core * half, half), half)
    mine, other = feats.at[x, rows, :], feats.at[1 - x, rows, :]
    spot = region(core, x, y, z)
    send(other, spot, x_send, x_recv, across)
    send(mine, spot, y_send.at[0], y_recv.at[0], beside)
    for d in (1, 2, 3):
        send(mine, spot, z_send.at[d - 1], z_recv.at[d - 1], dev(core, x, y, far[d - 1]))
    send(mine, spot, b_send.at[0], b_recv.at[0], sibling)
    keep(mine, spot, l_sem.at[0])
    send(gain, gains.at[core], g_send, g_recv, sibling)
    keep(gain, gains.at[core], l_sem.at[1])

    far_x = region(core, 1 - x, y, z)
    remote(mine, far_x, x_send, x_recv, sibling).wait_recv()
    send(far_x, far_x, y_send.at[4], y_recv.at[4], beside)
    for d in (1, 2, 3):
        send(far_x, far_x, z_send.at[2 + d], z_recv.at[2 + d], dev(core, x, y, far[d - 1]))
    send(far_x, far_x, b_send.at[8], b_recv.at[8], sibling)

    def head_columns(zz, c):
        return w_qkv.at[0, :, :, pl.ds(pl.multiple_of((zz * 2 + c) * HD, HD), HD)]

    def depth_rows(c, xx, zz):
        return wq.at[c, :, pl.ds(pl.multiple_of((zz * 2 + xx) * depth, depth), depth), :]

    own_rows = depth_rows(core, x, z)
    for d in range(4):
        zz = z_apart(z, d)
        for other_core in range(2):
            target = 1 - core if other_core else core
            if d == 0 and not other_core:
                keep(head_columns(z, core), own_rows, l_sem.at[2])
                send(head_columns(z, core), own_rows, qx_send.at[0], qx_recv.at[0], across)
            else:
                at = 2 * d + other_core
                send(head_columns(zz, target), own_rows, q_send.at[at], q_recv.at[at], dev(target, x, y, zz))

    for k in range(2):
        xx = 1 - x if k else x
        for d in (1, 2, 3):
            got = region(core, xx, y, far[d - 1])
            remote(mine, got, x_send, z_recv.at[3 * k + d - 1], sibling).wait_recv()
            send(got, got, y_send.at[4 * k + d], y_recv.at[4 * k + d], beside)
            send(got, got, b_send.at[8 * k + d], b_recv.at[8 * k + d], sibling)
    half_rows = w_out.shape[1]
    to = wo.at[core, pl.ds(pl.multiple_of(y * half_rows, half_rows), half_rows), :]
    projections = []
    for a in range(2):
        for b in range(2):
            xx = 1 - x if a else x
            cc = 1 - core if b else core
            src = w_out.at[0, :, pl.ds(pl.multiple_of(cc * HD, HD), HD)]
            rsem = o_recv.at[2 * y + core]
            copy = remote(src, to, o_send.at[2 * a + b], rsem, dev(cc, xx, x, z))
            if a == 0 and b == 0:
                pl.when(x != y)(copy.start)
                pl.when(x == y)(pltpu.make_async_copy(src, to, rsem).start)
            else:
                copy.start()
            projections.append(copy)

    for d in range(4):
        for other_core in range(2):
            at = 2 * d + other_core
            if at == 0:
                continue
            got = depth_rows(1 - core if other_core else core, x, z_apart(z, d))
            remote(head_columns(z, core), got, x_send, q_recv.at[at], sibling).wait_recv()
            send(got, got, qx_send.at[at], qx_recv.at[at], across)
    for k in range(2):
        xx = 1 - x if k else x
        for d in range(4):
            got = region(core, xx, 1 - y, z_apart(z, d))
            remote(mine, got, x_send, y_recv.at[4 * k + d], sibling).wait_recv()
            send(got, got, b_send.at[8 * k + 4 + d], b_recv.at[8 * k + 4 + d], sibling)
    for k in range(2):
        xx = 1 - x if k else x
        for d in range(8):
            got = region(1 - core, xx, y if d < 4 else 1 - y, z_apart(z, d % 4))
            remote(mine, got, x_send, b_recv.at[8 * k + d], sibling).wait_recv()
    for d in range(4):
        for other_core in range(2):
            at = 2 * d + other_core
            got = depth_rows(1 - core if other_core else core, 1 - x, z_apart(z, d))
            remote(head_columns(z, core), got, x_send, qx_recv.at[at], sibling).wait_recv()
    remote(gain, gains.at[1 - core], g_send, g_recv, sibling).wait_recv()
    for yy in range(2):
        for cc in range(2):
            got = wo.at[cc, pl.ds(yy * half_rows, half_rows), :]
            remote(w_out.at[0, :, pl.ds(0, HD)], got, x_send, o_recv.at[2 * yy + cc], sibling).wait_recv()
    for copy in sent:
        copy.wait_send()
    for copy in local:
        copy.wait()
    pl.when(x != y)(projections[0].wait_send)
    for copy in projections[1:]:
        copy.wait_send()


def spread(feats, gain, w_qkv, w_out):
    dma = pltpu.SemaphoreType.DMA
    bf = jnp.bfloat16
    rows, wide = feats.shape[1] * 8, feats.shape[2] * 2
    return pl.pallas_call(
        spread_kernel,
        out_shape=(
            jax.ShapeDtypeStruct((rows, wide), bf),
            jax.ShapeDtypeStruct((2, 1, wide), jnp.float32),
            jax.ShapeDtypeStruct((2, 3, wide, HD), bf),
            jax.ShapeDtypeStruct((2, wide, HD), bf),
        ),
        in_specs=[ANY] * 4,
        out_specs=(ANY,) * 4,
        scratch_shapes=[dma((3,)), dma(()), dma(()), dma((6,)), dma((6,)), dma((8,)), dma((8,)), dma((16,)), dma((16,)),
                        dma(()), dma(()), dma((8,)), dma((8,)), dma((8,)), dma((8,)), dma((4,)), dma((4,))],
        compiler_params=pltpu.CompilerParams(collective_id=0, has_side_effects=True),
        name="spread",
    )(feats, gain, w_qkv, w_out)


def deliver_kernel(mid, last, out, l_sem, m_send, m_recv, a_send, a_recv):
    core, x, y, z = place()
    node = z * 2 + x
    rows, wide = out.shape[1], out.shape[2]
    piece = last.shape[1]
    to_y = lax.div(z, 2)
    z_low = lax.rem(z, 2)
    first = core == 0
    to_self = (core == 1) & (y == to_y)
    barrier = pltpu.get_barrier_semaphore()

    def signal(peer):
        pl.semaphore_signal(barrier, inc=1, device_id=peer, device_id_type=MESH_ID)

    @pl.when(first)
    def _():
        signal(dev(0, 1 - x, y, z))

    sources = [(zl, xx, yy, cc) for zl in range(2) for xx in range(2) for yy in range(2) for cc in range(2)]
    for zl, xx, yy, cc in sources:
        own = (cc == core) & (xx == x) & (yy == y) & (2 * y + zl == z)

        @pl.when((core == 1) & jnp.logical_not(own))
        def _():
            signal(dev(cc, xx, yy, 2 * y + zl))

    pl.semaphore_wait(barrier, 8 - to_self.astype(jnp.int32) + first.astype(jnp.int32))

    def mid_rows(n):
        return mid.at[
            pl.ds(pl.multiple_of(n * rows, rows), rows), pl.ds(pl.multiple_of(y * wide, wide), wide)
        ]

    cross = remote(mid_rows(z * 2 + 1 - x), out.at[x], m_send, m_recv, dev(0, 1 - x, y, z))
    keep = pltpu.make_async_copy(mid_rows(node), out.at[x], l_sem)

    @pl.when(first)
    def _():
        cross.start()
        keep.start()

    slot = 4 * z_low + 2 * y + core
    spot = out.at[x, :, pl.ds(pl.multiple_of(slot * piece, piece), piece)]
    index = 8 * z_low + 4 * x + 2 * y + core
    copies = []
    for n in range(8):
        src = last.at[pl.ds(n * rows, rows), :]
        copy = remote(src, spot, a_send.at[n], a_recv.at[index], dev(1, n % 2, to_y, n // 2))
        own = to_self & (node == n)
        pl.when(jnp.logical_not(own))(copy.start)
        pl.when(own)(pltpu.make_async_copy(src, spot, a_recv.at[index]).start)
        copies.append((copy, own))

    @pl.when(first)
    def _():
        remote(mid_rows(node), out.at[1 - x], m_send, m_recv, dev(0, 1 - x, y, z)).wait_recv()
        cross.wait_send()
        keep.wait()

    @pl.when(core == 1)
    def _():
        for zl, xx, yy, cc in sources:
            at = 4 * zl + 2 * yy + cc
            got = out.at[xx, :, pl.ds(at * piece, piece)]
            remote(
                last.at[pl.ds(0, rows), :], got, a_send.at[0], a_recv.at[8 * zl + 4 * xx + 2 * yy + cc],
                dev(0, x, y, z),
            ).wait_recv()

    for copy, own in copies:
        pl.when(jnp.logical_not(own))(copy.wait_send)


def deliver(mid, last):
    dma = pltpu.SemaphoreType.DMA
    return pl.pallas_call(
        deliver_kernel,
        out_shape=jax.ShapeDtypeStruct((2, mid.shape[0] // 8, mid.shape[1] // 2), mid.dtype),
        in_specs=[ANY] * 2,
        out_specs=ANY,
        scratch_shapes=[dma(()), dma(()), dma(()), dma((8,)), dma((16,))],
        compiler_params=pltpu.CompilerParams(collective_id=3, has_side_effects=True),
        name="deliver",
    )(mid, last)


def attend_kernel(x_ref, gain_ref, w_ref, flags, out_ref, q_ref, k_ref, v_ref):
    count = flags.shape[0]
    step = x_ref.shape[0]
    rows = q_ref.shape[0] // count
    width = count.bit_length() - 1
    bits = [width - 1, width // 2, 0]
    at = pl.program_id(0)
    here = pl.ds(pl.multiple_of(at * step, step), step)
    xf = x_ref[...].astype(jnp.float32)
    inv = lax.rsqrt(jnp.mean(xf * xf, axis=-1, keepdims=True) + EPS)
    normed = (xf * inv * gain_ref[0]).astype(jnp.bfloat16)
    for part, ref in enumerate((q_ref, k_ref, v_ref)):
        ref[here, :] = jnp.dot(normed, w_ref[0, part], preferred_element_type=jnp.float32).astype(jnp.bfloat16)

    @pl.when(at == pl.num_programs(0) - 1)
    def _():
        for block in range(count):
            seen = [block] + [block ^ (1 << bit) for bit in bits]
            span = slice(block * rows, (block + 1) * rows)
            query = q_ref[span, :]
            scores = []
            for other in seen:
                key = k_ref[other * rows : (other + 1) * rows, :]
                dots = lax.dot_general(query, key, (((1,), (1,)), ((), ())), preferred_element_type=jnp.float32)
                scores.append(jnp.where(flags[block, other] > 0, dots * (1.0 / HD**0.5), NEG))
            top = functools.reduce(jnp.maximum, [jnp.max(s, axis=-1, keepdims=True) for s in scores])
            total = jnp.zeros_like(top)
            summed = jnp.zeros((rows, HD), jnp.float32)
            for other, s in zip(seen, scores):
                expo = jnp.where(flags[block, other] > 0, jnp.exp(s - top), 0.0)
                total = total + jnp.sum(expo, axis=-1, keepdims=True)
                summed = summed + jnp.dot(
                    expo.astype(jnp.bfloat16), v_ref[other * rows : (other + 1) * rows, :],
                    preferred_element_type=jnp.float32,
                )
            out_ref[span, :] = (summed / total).astype(jnp.bfloat16)


def attend(x, gains, w, flags, s):
    rows, wide = x.shape
    step = rows // 4
    return pl.pallas_call(
        attend_kernel,
        grid=(4,),
        out_shape=jax.ShapeDtypeStruct((rows, HD), jnp.bfloat16),
        in_specs=[
            pl.BlockSpec((step, wide), lambda i: (i, 0)),
            pl.BlockSpec((1, 1, wide), lambda i: (s, 0, 0)),
            pl.BlockSpec((1, 3, wide, HD), lambda i: (s, 0, 0, 0)),
            pl.BlockSpec(memory_space=pltpu.SMEM),
        ],
        out_specs=pl.BlockSpec((rows, HD), lambda i: (0, 0)),
        scratch_shapes=[pltpu.VMEM((rows, HD), jnp.bfloat16)] * 3,
        compiler_params=pltpu.CompilerParams(vmem_limit_bytes=40 * 2**20),
        name="attend",
    )(x, gains, w, flags)


def local_planes(feats, gain, w_qkv, w_out, block_mask):
    core, micro, y, z = place()
    flags = lax.dynamic_index_in_dim(block_mask, micro, 0, keepdims=False)
    whole, gains, wq, wo = spread(feats, gain, w_qkv, w_out)
    column = column_slot(core, y, z) * HD

    def layer(x, s):
        attended = all_columns(attend(x, gains, wq, flags, s), head_slot, 1)
        projected = jnp.dot(attended, wo[s], preferred_element_type=jnp.float32)
        residual = lax.dynamic_slice_in_dim(x, column, HD, axis=1)
        return (residual.astype(jnp.float32) + projected).astype(jnp.bfloat16)

    mid = all_columns(layer(whole, 0), column_slot, 2)
    return deliver(mid, layer(mid, 1))[None]


def solution(mesh):
    planes = (mesh.shape["pipe"], mesh.shape["node"], mesh.shape["head"]) == (2, 8, 2)
    return jax.shard_map(
        local_planes if planes else local_any,
        mesh=mesh,
        in_specs=(
            P(None, "node", "head"),
            P("pipe", None),
            P("pipe", None, "node", "head"),
            P("pipe", "head", "node"),
            P(),
        ),
        out_specs=P("pipe", None, "node", "head"),
        check_vma=False,
    )
```

```python
import functools
import jax
import jax.numpy as jnp
from jax import lax
from jax.experimental import pallas as pl
from jax.experimental.pallas import tpu as pltpu
from jax.sharding import PartitionSpec as P

HD = 128
MICRO = 2


EPS = 1e-06
NEG = -1e30


def from_partner(block, axis, apart):
    count = lax.axis_size(axis)
    route = []
    for low in range(count):
        high = low | 1 << apart
        if high != low and high < count:
            route += [(low, high), (high, low)]
    return lax.ppermute(block, axis, route)


def from_behind(value, axis, steps):
    count = lax.axis_size(axis)
    first, last = (max(0, -steps), min(count, count - steps))
    return lax.ppermute(value, axis, [(source, source + steps) for source in range(first, last)])


def partial_attend(query, key, value, keep):
    rows = query.shape[0]
    groups = query.shape[1] // HD
    q_heads = query.reshape(rows, groups, HD)
    k_heads = key.reshape(key.shape[0], groups, HD)
    v_heads = value.reshape(value.shape[0], groups, HD)
    scores = jnp.einsum("qhd,khd->hqk", q_heads, k_heads, preferred_element_type=jnp.float32) * (
        1.0 / HD**0.5
    )
    scores = jnp.where(keep[None, None, :], scores, NEG)
    top = jnp.max(scores, axis=-1)
    expo = jnp.where(keep[None, None, :], jnp.exp(scores - top[..., None]), 0.0)
    total = jnp.sum(expo, axis=-1)
    summed = jnp.einsum(
        "hqk,khd->hqd", expo.astype(jnp.bfloat16), v_heads, preferred_element_type=jnp.float32
    )
    return (summed, top, total)


def finish(summed, total):
    out = summed / total[..., None]
    rows = out.shape[1]
    return jnp.transpose(out, (1, 0, 2)).reshape(rows, -1).astype(jnp.bfloat16)


def local_any(feats, gain, w_qkv, w_out, block_mask):
    segment = lax.axis_index("pipe")
    me = lax.axis_index("node")
    width = lax.axis_size("node").bit_length() - 1
    bit_list = [width - 1, width // 2, 0]
    qkv_whole, out_whole = (
        lax.all_gather(w_qkv, "node", axis=2, tiled=True),
        lax.all_gather(w_out, "node", axis=2, tiled=True),
    )
    w_query = qkv_whole[0, 0]
    w_key = qkv_whole[0, 1]
    w_value = qkv_whole[0, 2]
    w_proj = out_whole[0]
    gain_row = gain[0]
    rows = feats.shape[1]
    carried = jnp.zeros_like(feats[0])
    results = []
    for tick in range(MICRO + 1):
        micro = jnp.clip(tick - segment, 0, MICRO - 1)
        fresh = feats[min(tick, MICRO - 1)]
        inputs = jnp.where(segment == 0, fresh, carried)
        whole = lax.all_gather(inputs, "head", axis=1, tiled=True)
        xf = whole.astype(jnp.float32)
        inv = lax.rsqrt(jnp.mean(xf * xf, axis=-1, keepdims=True) + EPS)
        normed = (xf * inv * gain_row).astype(jnp.bfloat16)
        query = jnp.dot(normed, w_query, preferred_element_type=jnp.float32).astype(jnp.bfloat16)
        key = jnp.dot(normed, w_key, preferred_element_type=jnp.float32).astype(jnp.bfloat16)
        value = jnp.dot(normed, w_value, preferred_element_type=jnp.float32).astype(jnp.bfloat16)
        mask_rows = lax.dynamic_index_in_dim(block_mask, micro, 0, keepdims=False)
        own_flag = mask_rows[me, me] > 0
        key_list = [key]
        value_list = [value]
        flag_list = [own_flag]
        for bit in bit_list:
            far_key, far_value = from_partner((key, value), "node", bit)
            key_list.append(far_key)
            value_list.append(far_value)
            flag_list.append(mask_rows[me, jnp.bitwise_xor(me, 1 << bit)] > 0)
        keep = jnp.repeat(jnp.stack(flag_list), rows)
        summed, top, total = partial_attend(
            query, jnp.concatenate(key_list, 0), jnp.concatenate(value_list, 0), keep
        )
        attended = finish(summed, total)
        terms = jnp.dot(attended, w_proj, preferred_element_type=jnp.float32)
        reduced = lax.psum_scatter(
            terms.astype(jnp.bfloat16), "head", scatter_dimension=1, tiled=True
        ).astype(jnp.float32)
        output = (inputs.astype(jnp.float32) + reduced).astype(jnp.bfloat16)
        results.append(output)
        if tick < MICRO:
            carried = from_behind(output, "pipe", 1)
    first = jnp.where(segment == 0, results[0], results[1])
    second = jnp.where(segment == 0, results[1], results[2])
    return jnp.stack([first, second])[None]


PIECES = 4
MESH_ID = pl.DeviceIdType.MESH
ANY = pl.BlockSpec(memory_space=pl.ANY)


def place():
    core, node, y = lax.axis_index("pipe"), lax.axis_index("node"), lax.axis_index("head")
    return core, lax.rem(node, 2), y, lax.div(node, 2)


def dev(core, x, y, z):
    return (core, z * 2 + x, y)


def z_apart(z, d):
    if d == 0:
        return z
    if d == 1:
        return z + 1 - 2 * lax.rem(z, 2)
    if d == 2:
        return z + 2 - 4 * lax.div(z, 2)
    return 3 - z


def remote(src, dst, send, recv, target):
    return pltpu.make_async_remote_copy(
        src_ref=src, dst_ref=dst, send_sem=send, recv_sem=recv, device_id=target, device_id_type=MESH_ID
    )


def greet(peers):
    barrier = pltpu.get_barrier_semaphore()
    for peer in peers:
        pl.semaphore_signal(barrier, inc=1, device_id=peer, device_id_type=MESH_ID)
    pl.semaphore_wait(barrier, len(peers))


def head_slot(core, y, z):
    return 8 * y + 2 * z + core


def column_slot(core, y, z):
    return 4 * z + 2 * y + core


class Gather:
    def __init__(self, slot, own, out, sems, sent):
        self.slot, self.own, self.out, self.sent = slot, own, out, sent
        self.local, self.zs, self.zr, self.ys, self.yr, self.bs, self.br = sems
        self.at = place()
        self.rows, self.wide = own.shape[0] // PIECES, own.shape[1]
        core, x, y, z = self.at
        self.far = [dev(core, x, y, z_apart(z, d)) for d in (1, 2, 3)]
        self.beside, self.sibling = dev(core, x, 1 - y, z), dev(1 - core, x, y, z)

    def peers(self):
        return self.far + [self.beside, self.sibling]

    def mine(self, p):
        return self.own.at[pl.ds(p * self.rows, self.rows), :]

    def region(self, c, yy, zz, p):
        column = pl.multiple_of(self.slot(c, yy, zz) * self.wide, self.wide)
        return self.out.at[pl.ds(p * self.rows, self.rows), pl.ds(column, self.wide)]

    def send(self, src, dst, ssem, rsem, target):
        copy = remote(src, dst, ssem, rsem, target)
        copy.start()
        self.sent.append(copy.wait_send)

    def await_recv(self, got, sem):
        remote(self.mine(0), got, sem, sem, self.sibling).wait_recv()

    def start(self, p):
        core, x, y, z = self.at
        mine, spot = self.mine(p), self.region(core, y, z, p)
        for d in (1, 2, 3):
            self.send(mine, spot, self.zs.at[p, d - 1], self.zr.at[p, d - 1], self.far[d - 1])
        self.send(mine, spot, self.ys.at[p, 0], self.yr.at[p, 0], self.beside)
        self.send(mine, spot, self.bs.at[p, 0], self.br.at[p, 0], self.sibling)
        pltpu.make_async_copy(mine, spot, self.local.at[p]).start()

    def along_z(self, p):
        core, x, y, z = self.at
        for d in (1, 2, 3):
            got = self.region(core, y, z_apart(z, d), p)
            self.await_recv(got, self.zr.at[p, d - 1])
            self.send(got, got, self.ys.at[p, d], self.yr.at[p, d], self.beside)
            self.send(got, got, self.bs.at[p, d], self.br.at[p, d], self.sibling)

    def along_y(self, p):
        core, x, y, z = self.at
        for d in range(4):
            got = self.region(core, 1 - y, z_apart(z, d), p)
            self.await_recv(got, self.yr.at[p, d])
            self.send(got, got, self.bs.at[p, 4 + d], self.br.at[p, 4 + d], self.sibling)

    def whole(self, p):
        core, x, y, z = self.at
        for d in range(8):
            got = self.region(1 - core, y if d < 4 else 1 - y, z_apart(z, d % 4), p)
            self.await_recv(got, self.br.at[p, d])
        pltpu.make_async_copy(self.mine(p), self.region(core, y, z, p), self.local.at[p]).wait()


def gather_sems():
    dma = pltpu.SemaphoreType.DMA
    return [dma((PIECES,))] + [dma((PIECES, c)) for c in (3, 3, 4, 4, 8, 8)]


def own_columns(array):
    core, x, y, z = place()
    return array.at[:, pl.ds(pl.multiple_of(column_slot(core, y, z) * HD, HD), HD)]


def project_piece(all_ref, wo_ref, s, rest_ref, into_ref, p):
    rows = all_ref.shape[0] // PIECES
    span = slice(p * rows, (p + 1) * rows)
    projected = jnp.dot(all_ref[span, :], wo_ref[s], preferred_element_type=jnp.float32)
    into_ref[span, :] = (rest_ref[span, :].astype(jnp.float32) + projected).astype(jnp.bfloat16)


def turn_kernel(
    own, x, wo_ref, gain_ref, w_ref, flags, mid, out_ref,
    all_ref, rest_ref, into_ref, q_ref, k_ref, v_ref, rest_sem, *sems,
):
    sent = []
    heads = Gather(head_slot, own, all_ref, sems[:7], sent)
    columns = Gather(column_slot, into_ref, mid, sems[7:], sent)
    greet(heads.peers())
    for p in range(PIECES):
        heads.start(p)
    rest = pltpu.make_async_copy(own_columns(x), rest_ref, rest_sem)
    rest.start()
    rest.wait()
    rows = mid.shape[0] // PIECES
    for step in range(2 * PIECES + 2):
        for stage in range(3):
            part = step - stage
            if part < 0 or part >= 2 * PIECES:
                continue
            gather, p = (heads, part) if part < PIECES else (columns, part - PIECES)
            if stage == 0:
                gather.along_z(p)
            elif stage == 1:
                gather.along_y(p)
            else:
                gather.whole(p)
                if gather is heads:
                    project_piece(all_ref, wo_ref, 0, rest_ref, into_ref, p)
                    columns.start(p)
                else:
                    span = pl.ds(p * rows, rows)
                    project_rows(
                        mid[span, :].astype(jnp.float32), gain_ref[1], lambda part: w_ref[1, part],
                        (q_ref, k_ref, v_ref), span,
                    )
    attend_blocks(q_ref, k_ref, v_ref, flags, out_ref)
    for wait in sent:
        wait()


def turn(own, x, wo, gains, w, flags):
    dma = pltpu.SemaphoreType.DMA
    vmem = pl.BlockSpec(memory_space=pltpu.VMEM)
    rows, wide = x.shape
    narrow = pltpu.VMEM((rows, HD), jnp.bfloat16)
    return pl.pallas_call(
        turn_kernel,
        out_shape=(jax.ShapeDtypeStruct((rows, wide), x.dtype), jax.ShapeDtypeStruct((rows, HD), x.dtype)),
        in_specs=[ANY, ANY, vmem, vmem, vmem, pl.BlockSpec(memory_space=pltpu.SMEM)],
        out_specs=(vmem, vmem),
        scratch_shapes=[pltpu.VMEM((rows, wide), jnp.bfloat16)] + [narrow] * 5 + [dma(())]
        + gather_sems() + gather_sems(),
        compiler_params=pltpu.CompilerParams(
            collective_id=1, has_side_effects=True, vmem_limit_bytes=48 * 2**20
        ),
        name="turn",
    )(own, x, wo, gains, w, flags)


def spread_kernel(
    feats, gain, w_qkv, w_out, xg, gains, wq, wo,
    l_sem, x_send, x_recv, z_send, z_recv, y_send, y_recv, b_send, b_recv,
    g_send, g_recv, q_send, q_recv, qx_send, qx_recv, o_send, o_recv,
):
    core, x, y, z = place()
    node = z * 2 + x
    half, wide = feats.shape[1] // 2, feats.shape[2]
    depth = w_qkv.shape[2]
    far = [z_apart(z, d) for d in (1, 2, 3)]
    beside, sibling, across = dev(core, x, 1 - y, z), dev(1 - core, x, y, z), dev(core, 1 - x, y, z)
    plane = [
        dev(cc, xx, yy, z)
        for cc in (core, 1 - core)
        for xx in (x, 1 - x)
        for yy in (y, 1 - y)
    ][1:]
    greet(plane + [dev(cc, x, y, zz) for zz in far for cc in (core, 1 - core)])
    sent = []
    local = []

    def send(src, dst, ssem, rsem, target):
        copy = remote(src, dst, ssem, rsem, target)
        copy.start()
        sent.append(copy)

    def keep(src, dst, sem):
        copy = pltpu.make_async_copy(src, dst, sem)
        copy.start()
        local.append(copy)

    def region(c, xx, yy, zz):
        return xg.at[
            pl.ds(pl.multiple_of((zz * 2 + xx) * 2 * half + c * half, half), half),
            pl.ds(pl.multiple_of(yy * wide, wide), wide),
        ]

    rows = pl.ds(pl.multiple_of(core * half, half), half)
    mine, other = feats.at[x, rows, :], feats.at[1 - x, rows, :]
    spot = region(core, x, y, z)
    send(other, spot, x_send, x_recv, across)
    send(mine, spot, y_send.at[0], y_recv.at[0], beside)
    for d in (1, 2, 3):
        send(mine, spot, z_send.at[d - 1], z_recv.at[d - 1], dev(core, x, y, far[d - 1]))
    send(mine, spot, b_send.at[0], b_recv.at[0], sibling)
    keep(mine, spot, l_sem.at[0])
    send(gain, gains.at[core], g_send, g_recv, sibling)
    keep(gain, gains.at[core], l_sem.at[1])

    far_x = region(core, 1 - x, y, z)
    remote(mine, far_x, x_send, x_recv, sibling).wait_recv()
    send(far_x, far_x, y_send.at[4], y_recv.at[4], beside)
    for d in (1, 2, 3):
        send(far_x, far_x, z_send.at[2 + d], z_recv.at[2 + d], dev(core, x, y, far[d - 1]))
    send(far_x, far_x, b_send.at[8], b_recv.at[8], sibling)

    def head_columns(zz, c):
        return w_qkv.at[0, :, :, pl.ds(pl.multiple_of((zz * 2 + c) * HD, HD), HD)]

    def depth_rows(c, xx, zz):
        return wq.at[c, :, pl.ds(pl.multiple_of((zz * 2 + xx) * depth, depth), depth), :]

    own_rows = depth_rows(core, x, z)
    for d in range(4):
        zz = z_apart(z, d)
        for other_core in range(2):
            target = 1 - core if other_core else core
            if d == 0 and not other_core:
                keep(head_columns(z, core), own_rows, l_sem.at[2])
                send(head_columns(z, core), own_rows, qx_send.at[0], qx_recv.at[0], across)
            else:
                at = 2 * d + other_core
                send(head_columns(zz, target), own_rows, q_send.at[at], q_recv.at[at], dev(target, x, y, zz))

    for k in range(2):
        xx = 1 - x if k else x
        for d in (1, 2, 3):
            got = region(core, xx, y, far[d - 1])
            remote(mine, got, x_send, z_recv.at[3 * k + d - 1], sibling).wait_recv()
            send(got, got, y_send.at[4 * k + d], y_recv.at[4 * k + d], beside)
            send(got, got, b_send.at[8 * k + d], b_recv.at[8 * k + d], sibling)
    half_rows = w_out.shape[1]
    to = wo.at[core, pl.ds(pl.multiple_of(y * half_rows, half_rows), half_rows), :]
    projections = []
    for a in range(2):
        for b in range(2):
            xx = 1 - x if a else x
            cc = 1 - core if b else core
            src = w_out.at[0, :, pl.ds(pl.multiple_of(cc * HD, HD), HD)]
            rsem = o_recv.at[2 * y + core]
            copy = remote(src, to, o_send.at[2 * a + b], rsem, dev(cc, xx, x, z))
            if a == 0 and b == 0:
                pl.when(x != y)(copy.start)
                pl.when(x == y)(pltpu.make_async_copy(src, to, rsem).start)
            else:
                copy.start()
            projections.append(copy)

    for d in range(4):
        for other_core in range(2):
            at = 2 * d + other_core
            if at == 0:
                continue
            got = depth_rows(1 - core if other_core else core, x, z_apart(z, d))
            remote(head_columns(z, core), got, x_send, q_recv.at[at], sibling).wait_recv()
            send(got, got, qx_send.at[at], qx_recv.at[at], across)
    for k in range(2):
        xx = 1 - x if k else x
        for d in range(4):
            got = region(core, xx, 1 - y, z_apart(z, d))
            remote(mine, got, x_send, y_recv.at[4 * k + d], sibling).wait_recv()
            send(got, got, b_send.at[8 * k + 4 + d], b_recv.at[8 * k + 4 + d], sibling)
    for k in range(2):
        xx = 1 - x if k else x
        for d in range(8):
            got = region(1 - core, xx, y if d < 4 else 1 - y, z_apart(z, d % 4))
            remote(mine, got, x_send, b_recv.at[8 * k + d], sibling).wait_recv()
    for d in range(4):
        for other_core in range(2):
            at = 2 * d + other_core
            got = depth_rows(1 - core if other_core else core, 1 - x, z_apart(z, d))
            remote(head_columns(z, core), got, x_send, qx_recv.at[at], sibling).wait_recv()
    remote(gain, gains.at[1 - core], g_send, g_recv, sibling).wait_recv()
    for yy in range(2):
        for cc in range(2):
            got = wo.at[cc, pl.ds(yy * half_rows, half_rows), :]
            remote(w_out.at[0, :, pl.ds(0, HD)], got, x_send, o_recv.at[2 * yy + cc], sibling).wait_recv()
    for copy in sent:
        copy.wait_send()
    for copy in local:
        copy.wait()
    pl.when(x != y)(projections[0].wait_send)
    for copy in projections[1:]:
        copy.wait_send()


def spread(feats, gain, w_qkv, w_out):
    dma = pltpu.SemaphoreType.DMA
    bf = jnp.bfloat16
    rows, wide = feats.shape[1] * 8, feats.shape[2] * 2
    return pl.pallas_call(
        spread_kernel,
        out_shape=(
            jax.ShapeDtypeStruct((rows, wide), bf),
            jax.ShapeDtypeStruct((2, 1, wide), jnp.float32),
            jax.ShapeDtypeStruct((2, 3, wide, HD), bf),
            jax.ShapeDtypeStruct((2, wide, HD), bf),
        ),
        in_specs=[ANY] * 4,
        out_specs=(ANY,) * 4,
        scratch_shapes=[dma((3,)), dma(()), dma(()), dma((6,)), dma((6,)), dma((8,)), dma((8,)), dma((16,)), dma((16,)),
                        dma(()), dma(()), dma((8,)), dma((8,)), dma((8,)), dma((8,)), dma((4,)), dma((4,))],
        compiler_params=pltpu.CompilerParams(collective_id=0, has_side_effects=True),
        name="spread",
    )(feats, gain, w_qkv, w_out)


def finish_kernel(
    own, mid, wo_ref, out,
    all_ref, rest_ref, last, rest_sem, l_sem, m_send, m_recv, a_send, a_recv, *sems,
):
    sent = []
    heads = Gather(head_slot, own, all_ref, sems, sent)
    core, x, y, z = place()
    node = z * 2 + x
    rows, wide = out.shape[1], out.shape[2]
    piece = last.shape[1]
    to_y = lax.div(z, 2)
    z_low = lax.rem(z, 2)
    first = core == 0
    to_self = (core == 1) & (y == to_y)
    barrier = pltpu.get_barrier_semaphore()

    def signal(peer):
        pl.semaphore_signal(barrier, inc=1, device_id=peer, device_id_type=MESH_ID)

    for peer in heads.peers():
        signal(peer)

    @pl.when(first)
    def _():
        signal(dev(0, 1 - x, y, z))

    sources = [(zl, xx, yy, cc) for zl in range(2) for xx in range(2) for yy in range(2) for cc in range(2)]
    for zl, xx, yy, cc in sources:
        own = (cc == core) & (xx == x) & (yy == y) & (2 * y + zl == z)

        @pl.when((core == 1) & jnp.logical_not(own))
        def _():
            signal(dev(cc, xx, yy, 2 * y + zl))

    pl.semaphore_wait(barrier, 13 - to_self.astype(jnp.int32) + first.astype(jnp.int32))

    for p in range(PIECES):
        heads.start(p)
    rest = pltpu.make_async_copy(own_columns(mid), rest_ref, rest_sem)
    rest.start()

    def mid_rows(n):
        return mid.at[
            pl.ds(pl.multiple_of(n * rows, rows), rows), pl.ds(pl.multiple_of(y * wide, wide), wide)
        ]

    cross = remote(mid_rows(z * 2 + 1 - x), out.at[x], m_send, m_recv, dev(0, 1 - x, y, z))
    keep = pltpu.make_async_copy(mid_rows(node), out.at[x], l_sem)

    @pl.when(first)
    def _():
        cross.start()
        keep.start()

    slot = 4 * z_low + 2 * y + core
    spot = out.at[x, :, pl.ds(pl.multiple_of(slot * piece, piece), piece)]
    index = 8 * z_low + 4 * x + 2 * y + core
    copies = []
    rest.wait()
    for step in range(PIECES + 2):
        if step < PIECES:
            heads.along_z(step)
        if 0 <= step - 1 < PIECES:
            heads.along_y(step - 1)
        p = step - 2
        if p < 0:
            continue
        heads.whole(p)
        project_piece(all_ref, wo_ref, 1, rest_ref, last, p)
        for n in range(8 // PIECES * p, 8 // PIECES * (p + 1)):
            src = last.at[pl.ds(n * rows, rows), :]
            copy = remote(src, spot, a_send.at[n], a_recv.at[index], dev(1, n % 2, to_y, n // 2))
            mine = to_self & (node == n)
            pl.when(jnp.logical_not(mine))(copy.start)
            pl.when(mine)(pltpu.make_async_copy(src, spot, a_recv.at[index]).start)
            copies.append((copy, mine))

    @pl.when(first)
    def _():
        remote(mid_rows(node), out.at[1 - x], m_send, m_recv, dev(0, 1 - x, y, z)).wait_recv()
        cross.wait_send()
        keep.wait()

    @pl.when(core == 1)
    def _():
        for zl, xx, yy, cc in sources:
            at = 4 * zl + 2 * yy + cc
            got = out.at[xx, :, pl.ds(at * piece, piece)]
            remote(
                last.at[pl.ds(0, rows), :], got, a_send.at[0], a_recv.at[8 * zl + 4 * xx + 2 * yy + cc],
                dev(0, x, y, z),
            ).wait_recv()

    for copy, mine in copies:
        pl.when(jnp.logical_not(mine))(copy.wait_send)
    for wait in sent:
        wait()


def finish_layers(own, mid, wo):
    dma = pltpu.SemaphoreType.DMA
    rows, wide = mid.shape
    narrow = pltpu.VMEM((rows, HD), jnp.bfloat16)
    return pl.pallas_call(
        finish_kernel,
        out_shape=jax.ShapeDtypeStruct((2, rows // 8, wide // 2), mid.dtype),
        in_specs=[ANY, ANY, pl.BlockSpec(memory_space=pltpu.VMEM)],
        out_specs=ANY,
        scratch_shapes=[pltpu.VMEM((rows, wide), jnp.bfloat16), narrow, narrow]
        + [dma(()), dma(()), dma(()), dma(()), dma((8,)), dma((16,))] + gather_sems(),
        compiler_params=pltpu.CompilerParams(
            collective_id=3, has_side_effects=True, vmem_limit_bytes=40 * 2**20
        ),
        name="finish",
    )(own, mid, wo)


def project_rows(xf, gain_row, w_part, refs, here):
    inv = lax.rsqrt(jnp.mean(xf * xf, axis=-1, keepdims=True) + EPS)
    normed = (xf * inv * gain_row).astype(jnp.bfloat16)
    for part, ref in enumerate(refs):
        ref[here, :] = jnp.dot(normed, w_part(part), preferred_element_type=jnp.float32).astype(jnp.bfloat16)


def attend_blocks(q_ref, k_ref, v_ref, flags, out_ref):
    count = flags.shape[0]
    rows = q_ref.shape[0] // count
    width = count.bit_length() - 1
    bits = [width - 1, width // 2, 0]
    for block in range(count):
        seen = [block] + [block ^ (1 << bit) for bit in bits]
        span = slice(block * rows, (block + 1) * rows)
        query = q_ref[span, :]
        scores = []
        for other in seen:
            key = k_ref[other * rows : (other + 1) * rows, :]
            dots = lax.dot_general(query, key, (((1,), (1,)), ((), ())), preferred_element_type=jnp.float32)
            scores.append(jnp.where(flags[block, other] > 0, dots * (1.0 / HD**0.5), NEG))
        top = functools.reduce(jnp.maximum, [jnp.max(s, axis=-1, keepdims=True) for s in scores])
        total = jnp.zeros_like(top)
        summed = jnp.zeros((rows, HD), jnp.float32)
        for other, s in zip(seen, scores):
            expo = jnp.where(flags[block, other] > 0, jnp.exp(s - top), 0.0)
            total = total + jnp.sum(expo, axis=-1, keepdims=True)
            summed = summed + jnp.dot(
                expo.astype(jnp.bfloat16), v_ref[other * rows : (other + 1) * rows, :],
                preferred_element_type=jnp.float32,
            )
        out_ref[span, :] = (summed / total).astype(jnp.bfloat16)


def attend_kernel(x_ref, gain_ref, w_ref, flags, out_ref, q_ref, k_ref, v_ref):
    step = x_ref.shape[0]
    at = pl.program_id(0)
    here = pl.ds(pl.multiple_of(at * step, step), step)
    project_rows(
        x_ref[...].astype(jnp.float32), gain_ref[0], lambda part: w_ref[0, part], (q_ref, k_ref, v_ref), here
    )

    @pl.when(at == pl.num_programs(0) - 1)
    def _():
        attend_blocks(q_ref, k_ref, v_ref, flags, out_ref)


def attend(x, gains, w, flags, s):
    rows, wide = x.shape
    step = rows // 4
    return pl.pallas_call(
        attend_kernel,
        grid=(4,),
        out_shape=jax.ShapeDtypeStruct((rows, HD), jnp.bfloat16),
        in_specs=[
            pl.BlockSpec((step, wide), lambda i: (i, 0)),
            pl.BlockSpec((1, 1, wide), lambda i: (s, 0, 0)),
            pl.BlockSpec((1, 3, wide, HD), lambda i: (s, 0, 0, 0)),
            pl.BlockSpec(memory_space=pltpu.SMEM),
        ],
        out_specs=pl.BlockSpec((rows, HD), lambda i: (0, 0)),
        scratch_shapes=[pltpu.VMEM((rows, HD), jnp.bfloat16)] * 3,
        compiler_params=pltpu.CompilerParams(vmem_limit_bytes=40 * 2**20),
        name="attend",
    )(x, gains, w, flags)


def local_planes(feats, gain, w_qkv, w_out, block_mask):
    core, micro, y, z = place()
    flags = lax.dynamic_index_in_dim(block_mask, micro, 0, keepdims=False)
    whole, gains, wq, wo = spread(feats, gain, w_qkv, w_out)
    mid, attended = turn(attend(whole, gains, wq, flags, 0), whole, wo, gains, wq, flags)
    return finish_layers(attended, mid, wo)[None]


def solution(mesh):
    planes = (mesh.shape["pipe"], mesh.shape["node"], mesh.shape["head"]) == (2, 8, 2)
    return jax.shard_map(
        local_planes if planes else local_any,
        mesh=mesh,
        in_specs=(
            P(None, "node", "head"),
            P("pipe", None),
            P("pipe", None, "node", "head"),
            P("pipe", "head", "node"),
            P(),
        ),
        out_specs=P("pipe", None, "node", "head"),
        check_vma=False,
    )
```

```python
import functools
import jax
import jax.numpy as jnp
from jax import lax
from jax.experimental import pallas as pl
from jax.experimental.pallas import tpu as pltpu
from jax.sharding import PartitionSpec as P

HD = 128
MICRO = 2


EPS = 1e-06
NEG = -1e30


def from_partner(block, axis, apart):
    count = lax.axis_size(axis)
    route = []
    for low in range(count):
        high = low | 1 << apart
        if high != low and high < count:
            route += [(low, high), (high, low)]
    return lax.ppermute(block, axis, route)


def from_behind(value, axis, steps):
    count = lax.axis_size(axis)
    first, last = (max(0, -steps), min(count, count - steps))
    return lax.ppermute(value, axis, [(source, source + steps) for source in range(first, last)])


def partial_attend(query, key, value, keep):
    rows = query.shape[0]
    groups = query.shape[1] // HD
    q_heads = query.reshape(rows, groups, HD)
    k_heads = key.reshape(key.shape[0], groups, HD)
    v_heads = value.reshape(value.shape[0], groups, HD)
    scores = jnp.einsum("qhd,khd->hqk", q_heads, k_heads, preferred_element_type=jnp.float32) * (
        1.0 / HD**0.5
    )
    scores = jnp.where(keep[None, None, :], scores, NEG)
    top = jnp.max(scores, axis=-1)
    expo = jnp.where(keep[None, None, :], jnp.exp(scores - top[..., None]), 0.0)
    total = jnp.sum(expo, axis=-1)
    summed = jnp.einsum(
        "hqk,khd->hqd", expo.astype(jnp.bfloat16), v_heads, preferred_element_type=jnp.float32
    )
    return (summed, top, total)


def finish(summed, total):
    out = summed / total[..., None]
    rows = out.shape[1]
    return jnp.transpose(out, (1, 0, 2)).reshape(rows, -1).astype(jnp.bfloat16)


def local_any(feats, gain, w_qkv, w_out, block_mask):
    segment = lax.axis_index("pipe")
    me = lax.axis_index("node")
    width = lax.axis_size("node").bit_length() - 1
    bit_list = [width - 1, width // 2, 0]
    qkv_whole, out_whole = (
        lax.all_gather(w_qkv, "node", axis=2, tiled=True),
        lax.all_gather(w_out, "node", axis=2, tiled=True),
    )
    w_query = qkv_whole[0, 0]
    w_key = qkv_whole[0, 1]
    w_value = qkv_whole[0, 2]
    w_proj = out_whole[0]
    gain_row = gain[0]
    rows = feats.shape[1]
    carried = jnp.zeros_like(feats[0])
    results = []
    for tick in range(MICRO + 1):
        micro = jnp.clip(tick - segment, 0, MICRO - 1)
        fresh = feats[min(tick, MICRO - 1)]
        inputs = jnp.where(segment == 0, fresh, carried)
        whole = lax.all_gather(inputs, "head", axis=1, tiled=True)
        xf = whole.astype(jnp.float32)
        inv = lax.rsqrt(jnp.mean(xf * xf, axis=-1, keepdims=True) + EPS)
        normed = (xf * inv * gain_row).astype(jnp.bfloat16)
        query = jnp.dot(normed, w_query, preferred_element_type=jnp.float32).astype(jnp.bfloat16)
        key = jnp.dot(normed, w_key, preferred_element_type=jnp.float32).astype(jnp.bfloat16)
        value = jnp.dot(normed, w_value, preferred_element_type=jnp.float32).astype(jnp.bfloat16)
        mask_rows = lax.dynamic_index_in_dim(block_mask, micro, 0, keepdims=False)
        own_flag = mask_rows[me, me] > 0
        key_list = [key]
        value_list = [value]
        flag_list = [own_flag]
        for bit in bit_list:
            far_key, far_value = from_partner((key, value), "node", bit)
            key_list.append(far_key)
            value_list.append(far_value)
            flag_list.append(mask_rows[me, jnp.bitwise_xor(me, 1 << bit)] > 0)
        keep = jnp.repeat(jnp.stack(flag_list), rows)
        summed, top, total = partial_attend(
            query, jnp.concatenate(key_list, 0), jnp.concatenate(value_list, 0), keep
        )
        attended = finish(summed, total)
        terms = jnp.dot(attended, w_proj, preferred_element_type=jnp.float32)
        reduced = lax.psum_scatter(
            terms.astype(jnp.bfloat16), "head", scatter_dimension=1, tiled=True
        ).astype(jnp.float32)
        output = (inputs.astype(jnp.float32) + reduced).astype(jnp.bfloat16)
        results.append(output)
        if tick < MICRO:
            carried = from_behind(output, "pipe", 1)
    first = jnp.where(segment == 0, results[0], results[1])
    second = jnp.where(segment == 0, results[1], results[2])
    return jnp.stack([first, second])[None]


PIECES = 4
MESH_ID = pl.DeviceIdType.MESH
ANY = pl.BlockSpec(memory_space=pl.ANY)


def place():
    core, node, y = lax.axis_index("pipe"), lax.axis_index("node"), lax.axis_index("head")
    return core, lax.rem(node, 2), y, lax.div(node, 2)


def dev(core, x, y, z):
    return (core, z * 2 + x, y)


def z_apart(z, d):
    if d == 0:
        return z
    if d == 1:
        return z + 1 - 2 * lax.rem(z, 2)
    if d == 2:
        return z + 2 - 4 * lax.div(z, 2)
    return 3 - z


def remote(src, dst, send, recv, target):
    return pltpu.make_async_remote_copy(
        src_ref=src, dst_ref=dst, send_sem=send, recv_sem=recv, device_id=target, device_id_type=MESH_ID
    )


def greet(peers):
    barrier = pltpu.get_barrier_semaphore()
    for peer in peers:
        pl.semaphore_signal(barrier, inc=1, device_id=peer, device_id_type=MESH_ID)
    pl.semaphore_wait(barrier, len(peers))


def head_slot(core, y, z):
    return 8 * y + 2 * z + core


def column_slot(core, y, z):
    return 4 * z + 2 * y + core


class Gather:
    def __init__(self, slot, own, out, sems, sent):
        self.slot, self.own, self.out, self.sent = slot, own, out, sent
        self.local, self.zs, self.zr, self.ys, self.yr, self.bs, self.br = sems
        self.at = place()
        self.rows, self.wide = own.shape[0] // PIECES, own.shape[1]
        core, x, y, z = self.at
        self.far = [dev(core, x, y, z_apart(z, d)) for d in (1, 2, 3)]
        self.beside, self.sibling = dev(core, x, 1 - y, z), dev(1 - core, x, y, z)

    def peers(self):
        return self.far + [self.beside, self.sibling]

    def mine(self, p):
        return self.own.at[pl.ds(p * self.rows, self.rows), :]

    def region(self, c, yy, zz, p):
        column = pl.multiple_of(self.slot(c, yy, zz) * self.wide, self.wide)
        return self.out.at[pl.ds(p * self.rows, self.rows), pl.ds(column, self.wide)]

    def send(self, src, dst, ssem, rsem, target):
        copy = remote(src, dst, ssem, rsem, target)
        copy.start()
        self.sent.append(copy.wait_send)

    def await_recv(self, got, sem):
        remote(self.mine(0), got, sem, sem, self.sibling).wait_recv()

    def start(self, p):
        core, x, y, z = self.at
        mine, spot = self.mine(p), self.region(core, y, z, p)
        for d in (1, 2, 3):
            self.send(mine, spot, self.zs.at[p, d - 1], self.zr.at[p, d - 1], self.far[d - 1])
        self.send(mine, spot, self.ys.at[p, 0], self.yr.at[p, 0], self.beside)
        self.send(mine, spot, self.bs.at[p, 0], self.br.at[p, 0], self.sibling)
        pltpu.make_async_copy(mine, spot, self.local.at[p]).start()

    def along_z(self, p):
        core, x, y, z = self.at
        for d in (1, 2, 3):
            got = self.region(core, y, z_apart(z, d), p)
            self.await_recv(got, self.zr.at[p, d - 1])
            self.send(got, got, self.ys.at[p, d], self.yr.at[p, d], self.beside)
            self.send(got, got, self.bs.at[p, d], self.br.at[p, d], self.sibling)

    def along_y(self, p):
        core, x, y, z = self.at
        for d in range(4):
            got = self.region(core, 1 - y, z_apart(z, d), p)
            self.await_recv(got, self.yr.at[p, d])
            self.send(got, got, self.bs.at[p, 4 + d], self.br.at[p, 4 + d], self.sibling)

    def whole(self, p):
        core, x, y, z = self.at
        for d in range(8):
            got = self.region(1 - core, y if d < 4 else 1 - y, z_apart(z, d % 4), p)
            self.await_recv(got, self.br.at[p, d])
        pltpu.make_async_copy(self.mine(p), self.region(core, y, z, p), self.local.at[p]).wait()


def gather_sems():
    dma = pltpu.SemaphoreType.DMA
    return [dma((PIECES,))] + [dma((PIECES, c)) for c in (3, 3, 4, 4, 8, 8)]


def own_columns(array):
    core, x, y, z = place()
    return array.at[:, pl.ds(pl.multiple_of(column_slot(core, y, z) * HD, HD), HD)]


def project_piece(all_ref, wo_ref, s, rest_ref, into_ref, p):
    rows = all_ref.shape[0] // PIECES
    span = slice(p * rows, (p + 1) * rows)
    projected = jnp.dot(all_ref[span, :], wo_ref[s], preferred_element_type=jnp.float32)
    into_ref[span, :] = (rest_ref[span, :].astype(jnp.float32) + projected).astype(jnp.bfloat16)


def main_kernel(
    feats, gain, w_qkv, w_out, flags, mid, out_ref, wo,
    xg, gains, wq, all_ref, own, rest_ref, into_ref, q_ref, k_ref, v_ref,
    l_sem, x_send, x_recv, z_send, z_recv, y_send, y_recv, b_send, b_recv,
    g_send, g_recv, q_send, q_recv, qx_send, qx_recv, o_send, o_recv, rest_sem, *sems,
):
    core, x, y, z = place()
    node = z * 2 + x
    half, wide = feats.shape[1] // 2, feats.shape[2]
    depth = w_qkv.shape[2]
    far = [z_apart(z, d) for d in (1, 2, 3)]
    beside, sibling, across = dev(core, x, 1 - y, z), dev(1 - core, x, y, z), dev(core, 1 - x, y, z)
    plane = [
        dev(cc, xx, yy, z)
        for cc in (core, 1 - core)
        for xx in (x, 1 - x)
        for yy in (y, 1 - y)
    ][1:]
    greet(plane + [dev(cc, x, y, zz) for zz in far for cc in (core, 1 - core)])
    sent = []
    local = []

    def send(src, dst, ssem, rsem, target):
        copy = remote(src, dst, ssem, rsem, target)
        copy.start()
        sent.append(copy)

    def keep(src, dst, sem):
        copy = pltpu.make_async_copy(src, dst, sem)
        copy.start()
        local.append(copy)

    def region(c, xx, yy, zz):
        return xg.at[
            pl.ds(pl.multiple_of((zz * 2 + xx) * 2 * half + c * half, half), half),
            pl.ds(pl.multiple_of(yy * wide, wide), wide),
        ]

    rows = pl.ds(pl.multiple_of(core * half, half), half)
    mine, other = feats.at[x, rows, :], feats.at[1 - x, rows, :]
    spot = region(core, x, y, z)
    send(other, spot, x_send, x_recv, across)
    send(mine, spot, y_send.at[0], y_recv.at[0], beside)
    for d in (1, 2, 3):
        send(mine, spot, z_send.at[d - 1], z_recv.at[d - 1], dev(core, x, y, far[d - 1]))
    send(mine, spot, b_send.at[0], b_recv.at[0], sibling)
    keep(mine, spot, l_sem.at[0])
    send(gain, gains.at[core], g_send, g_recv, sibling)
    keep(gain, gains.at[core], l_sem.at[1])

    far_x = region(core, 1 - x, y, z)
    remote(mine, far_x, x_send, x_recv, sibling).wait_recv()
    send(far_x, far_x, y_send.at[4], y_recv.at[4], beside)
    for d in (1, 2, 3):
        send(far_x, far_x, z_send.at[2 + d], z_recv.at[2 + d], dev(core, x, y, far[d - 1]))
    send(far_x, far_x, b_send.at[8], b_recv.at[8], sibling)

    def head_columns(zz, c):
        return w_qkv.at[0, :, :, pl.ds(pl.multiple_of((zz * 2 + c) * HD, HD), HD)]

    def depth_rows(c, xx, zz):
        return wq.at[c, :, pl.ds(pl.multiple_of((zz * 2 + xx) * depth, depth), depth), :]

    own_rows = depth_rows(core, x, z)
    weights = []
    for d in range(4):
        zz = z_apart(z, d)
        for other_core in range(2):
            target = 1 - core if other_core else core
            if d == 0 and not other_core:
                keep(head_columns(z, core), own_rows, l_sem.at[2])
                weights.append(remote(head_columns(z, core), own_rows, qx_send.at[0], qx_recv.at[0], across))
            else:
                at = 2 * d + other_core
                weights.append(
                    remote(head_columns(zz, target), own_rows, q_send.at[at], q_recv.at[at], dev(target, x, y, zz))
                )

    def start_weights():
        for copy in weights:
            copy.start()

    def pass_section(s):
        for d in range(4):
            at = 2 * d + (core if s == 0 else 1 - core)
            got = depth_rows(s, x, z_apart(z, d))
            arrived = remote(head_columns(z, core), got, x_send, q_recv.at[at], sibling)
            if d:
                arrived.wait_recv()
                send(got, got, qx_send.at[at], qx_recv.at[at], across)
            else:
                copy = remote(got, got, qx_send.at[1], qx_recv.at[1], across)

                @pl.when(core != s)
                def _():
                    arrived.wait_recv()
                    copy.start()

                if s == 0:
                    weights.append(copy)

    def await_section(s):
        for d in range(4):
            at = 2 * d + (core if s == 0 else 1 - core)
            got = depth_rows(s, 1 - x, z_apart(z, d))
            remote(head_columns(z, core), got, x_send, qx_recv.at[at], sibling).wait_recv()

    def await_projection():
        for yy in range(2):
            for cc in range(2):
                got = wo.at[cc, pl.ds(yy * half_rows, half_rows), :]
                remote(w_out.at[0, :, pl.ds(0, HD)], got, x_send, o_recv.at[2 * yy + cc], sibling).wait_recv()

    pl.when(core == 0)(start_weights)
    for k in range(2):
        xx = 1 - x if k else x
        for d in (1, 2, 3):
            got = region(core, xx, y, far[d - 1])
            remote(mine, got, x_send, z_recv.at[3 * k + d - 1], sibling).wait_recv()
            send(got, got, y_send.at[4 * k + d], y_recv.at[4 * k + d], beside)
            send(got, got, b_send.at[8 * k + d], b_recv.at[8 * k + d], sibling)
    pl.when(core == 1)(start_weights)
    pass_section(0)
    for k in range(2):
        xx = 1 - x if k else x
        for d in range(4):
            got = region(core, xx, 1 - y, z_apart(z, d))
            remote(mine, got, x_send, y_recv.at[4 * k + d], sibling).wait_recv()
            send(got, got, b_send.at[8 * k + 4 + d], b_recv.at[8 * k + 4 + d], sibling)
    for k in range(2):
        xx = 1 - x if k else x
        for d in range(8):
            got = region(1 - core, xx, y if d < 4 else 1 - y, z_apart(z, d % 4))
            remote(mine, got, x_send, b_recv.at[8 * k + d], sibling).wait_recv()
    half_rows = w_out.shape[1]
    to = wo.at[core, pl.ds(pl.multiple_of(y * half_rows, half_rows), half_rows), :]
    projections = []
    for a in range(2):
        for b in range(2):
            xx = 1 - x if a else x
            cc = 1 - core if b else core
            src = w_out.at[0, :, pl.ds(pl.multiple_of(cc * HD, HD), HD)]
            rsem = o_recv.at[2 * y + core]
            copy = remote(src, to, o_send.at[2 * a + b], rsem, dev(cc, xx, x, z))
            if a == 0 and b == 0:
                pl.when(x != y)(copy.start)
                pl.when(x == y)(pltpu.make_async_copy(src, to, rsem).start)
            else:
                copy.start()
            projections.append(copy)

    remote(gain, gains.at[1 - core], g_send, g_recv, sibling).wait_recv()
    for copy in local:
        copy.wait()
    await_section(0)
    rest = pltpu.make_async_copy(own_columns(xg), rest_ref, rest_sem)
    rest.start()
    for p in range(PIECES):
        span = pl.ds(p * (xg.shape[0] // PIECES), xg.shape[0] // PIECES)
        project_rows(
            xg[span, :].astype(jnp.float32), gains[0], lambda part: wq[0, part], (q_ref, k_ref, v_ref), span
        )
    attend_blocks(q_ref, k_ref, v_ref, flags, own)
    rest.wait()
    waits = []
    heads = Gather(head_slot, own, all_ref, sems[:7], waits)
    columns = Gather(column_slot, into_ref, mid, sems[7:], waits)
    for p in range(PIECES):
        heads.start(p)
    pass_section(1)
    rows = mid.shape[0] // PIECES
    for step in range(2 * PIECES + 2):
        for stage in range(3):
            part = step - stage
            if part < 0 or part >= 2 * PIECES:
                continue
            gather, p = (heads, part) if part < PIECES else (columns, part - PIECES)
            if stage == 0:
                gather.along_z(p)
            elif stage == 1:
                gather.along_y(p)
            else:
                gather.whole(p)
                if part == 0:
                    await_projection()
                if part == PIECES:
                    await_section(1)
                if gather is heads:
                    project_piece(all_ref, wo, 0, rest_ref, into_ref, p)
                    columns.start(p)
                else:
                    span = pl.ds(p * rows, rows)
                    project_rows(
                        mid[span, :].astype(jnp.float32), gains[1], lambda part: wq[1, part],
                        (q_ref, k_ref, v_ref), span,
                    )
    attend_blocks(q_ref, k_ref, v_ref, flags, out_ref)
    for copy in sent + weights:
        copy.wait_send()
    pl.when(x != y)(projections[0].wait_send)
    for copy in projections[1:]:
        copy.wait_send()
    for wait in waits:
        wait()


def first_layer(feats, gain, w_qkv, w_out, flags):
    dma = pltpu.SemaphoreType.DMA
    vmem = pl.BlockSpec(memory_space=pltpu.VMEM)
    bf = jnp.bfloat16
    rows, wide = feats.shape[1] * 8, feats.shape[2] * 2
    narrow = pltpu.VMEM((rows, HD), bf)
    return pl.pallas_call(
        main_kernel,
        out_shape=(
            jax.ShapeDtypeStruct((rows, wide), bf),
            jax.ShapeDtypeStruct((rows, HD), bf),
            jax.ShapeDtypeStruct((2, wide, HD), bf),
        ),
        in_specs=[ANY] * 4 + [pl.BlockSpec(memory_space=pltpu.SMEM)],
        out_specs=(vmem,) * 3,
        scratch_shapes=[pltpu.VMEM((rows, wide), bf), pltpu.VMEM((2, 1, wide), jnp.float32),
                        pltpu.VMEM((2, 3, wide, HD), bf), pltpu.VMEM((rows, wide), bf)] + [narrow] * 6
        + [dma((3,)), dma(()), dma(()), dma((6,)), dma((6,)), dma((8,)), dma((8,)), dma((16,)), dma((16,)),
           dma(()), dma(()), dma((8,)), dma((8,)), dma((8,)), dma((8,)), dma((4,)), dma((4,)), dma(())]
        + gather_sems() + gather_sems(),
        compiler_params=pltpu.CompilerParams(
            collective_id=0, has_side_effects=True, vmem_limit_bytes=48 * 2**20
        ),
        name="first_layer",
    )(feats, gain, w_qkv, w_out, flags)


def finish_kernel(
    own, mid, wo_ref, out,
    all_ref, rest_ref, last, rest_sem, l_sem, m_send, m_recv, a_send, a_recv, *sems,
):
    sent = []
    heads = Gather(head_slot, own, all_ref, sems, sent)
    core, x, y, z = place()
    node = z * 2 + x
    rows, wide = out.shape[1], out.shape[2]
    piece = last.shape[1]
    to_y = lax.div(z, 2)
    z_low = lax.rem(z, 2)
    first = core == 0
    to_self = (core == 1) & (y == to_y)
    barrier = pltpu.get_barrier_semaphore()

    def signal(peer):
        pl.semaphore_signal(barrier, inc=1, device_id=peer, device_id_type=MESH_ID)

    for peer in heads.peers():
        signal(peer)

    @pl.when(first)
    def _():
        signal(dev(0, 1 - x, y, z))

    sources = [(zl, xx, yy, cc) for zl in range(2) for xx in range(2) for yy in range(2) for cc in range(2)]
    for zl, xx, yy, cc in sources:
        own = (cc == core) & (xx == x) & (yy == y) & (2 * y + zl == z)

        @pl.when((core == 1) & jnp.logical_not(own))
        def _():
            signal(dev(cc, xx, yy, 2 * y + zl))

    pl.semaphore_wait(barrier, 13 - to_self.astype(jnp.int32) + first.astype(jnp.int32))

    for p in range(PIECES):
        heads.start(p)
    rest = pltpu.make_async_copy(own_columns(mid), rest_ref, rest_sem)
    rest.start()

    def mid_rows(n):
        return mid.at[
            pl.ds(pl.multiple_of(n * rows, rows), rows), pl.ds(pl.multiple_of(y * wide, wide), wide)
        ]

    cross = remote(mid_rows(z * 2 + 1 - x), out.at[x], m_send, m_recv, dev(0, 1 - x, y, z))
    keep = pltpu.make_async_copy(mid_rows(node), out.at[x], l_sem)

    @pl.when(first)
    def _():
        cross.start()
        keep.start()

    slot = 4 * z_low + 2 * y + core
    spot = out.at[x, :, pl.ds(pl.multiple_of(slot * piece, piece), piece)]
    index = 8 * z_low + 4 * x + 2 * y + core
    copies = []
    rest.wait()
    for step in range(PIECES + 2):
        if step < PIECES:
            heads.along_z(step)
        if 0 <= step - 1 < PIECES:
            heads.along_y(step - 1)
        p = step - 2
        if p < 0:
            continue
        heads.whole(p)
        project_piece(all_ref, wo_ref, 1, rest_ref, last, p)
        for n in range(8 // PIECES * p, 8 // PIECES * (p + 1)):
            src = last.at[pl.ds(n * rows, rows), :]
            copy = remote(src, spot, a_send.at[n], a_recv.at[index], dev(1, n % 2, to_y, n // 2))
            mine = to_self & (node == n)
            pl.when(jnp.logical_not(mine))(copy.start)
            pl.when(mine)(pltpu.make_async_copy(src, spot, a_recv.at[index]).start)
            copies.append((copy, mine))

    @pl.when(first)
    def _():
        remote(mid_rows(node), out.at[1 - x], m_send, m_recv, dev(0, 1 - x, y, z)).wait_recv()
        cross.wait_send()
        keep.wait()

    @pl.when(core == 1)
    def _():
        for zl, xx, yy, cc in sources:
            at = 4 * zl + 2 * yy + cc
            got = out.at[xx, :, pl.ds(at * piece, piece)]
            remote(
                last.at[pl.ds(0, rows), :], got, a_send.at[0], a_recv.at[8 * zl + 4 * xx + 2 * yy + cc],
                dev(0, x, y, z),
            ).wait_recv()

    for copy, mine in copies:
        pl.when(jnp.logical_not(mine))(copy.wait_send)
    for wait in sent:
        wait()


def finish_layers(own, mid, wo):
    dma = pltpu.SemaphoreType.DMA
    rows, wide = mid.shape
    narrow = pltpu.VMEM((rows, HD), jnp.bfloat16)
    return pl.pallas_call(
        finish_kernel,
        out_shape=jax.ShapeDtypeStruct((2, rows // 8, wide // 2), mid.dtype),
        in_specs=[ANY, ANY, pl.BlockSpec(memory_space=pltpu.VMEM)],
        out_specs=ANY,
        scratch_shapes=[pltpu.VMEM((rows, wide), jnp.bfloat16), narrow, narrow]
        + [dma(()), dma(()), dma(()), dma(()), dma((8,)), dma((16,))] + gather_sems(),
        compiler_params=pltpu.CompilerParams(
            collective_id=3, has_side_effects=True, vmem_limit_bytes=40 * 2**20
        ),
        name="finish",
    )(own, mid, wo)


def project_rows(xf, gain_row, w_part, refs, here):
    inv = lax.rsqrt(jnp.mean(xf * xf, axis=-1, keepdims=True) + EPS)
    normed = (xf * inv * gain_row).astype(jnp.bfloat16)
    for part, ref in enumerate(refs):
        ref[here, :] = jnp.dot(normed, w_part(part), preferred_element_type=jnp.float32).astype(jnp.bfloat16)


def attend_blocks(q_ref, k_ref, v_ref, flags, out_ref):
    count = flags.shape[0]
    rows = q_ref.shape[0] // count
    width = count.bit_length() - 1
    bits = [width - 1, width // 2, 0]
    for block in range(count):
        seen = [block] + [block ^ (1 << bit) for bit in bits]
        span = slice(block * rows, (block + 1) * rows)
        query = q_ref[span, :]
        scores = []
        for other in seen:
            key = k_ref[other * rows : (other + 1) * rows, :]
            dots = lax.dot_general(query, key, (((1,), (1,)), ((), ())), preferred_element_type=jnp.float32)
            scores.append(jnp.where(flags[block, other] > 0, dots * (1.0 / HD**0.5), NEG))
        top = functools.reduce(jnp.maximum, [jnp.max(s, axis=-1, keepdims=True) for s in scores])
        total = jnp.zeros_like(top)
        summed = jnp.zeros((rows, HD), jnp.float32)
        for other, s in zip(seen, scores):
            expo = jnp.where(flags[block, other] > 0, jnp.exp(s - top), 0.0)
            total = total + jnp.sum(expo, axis=-1, keepdims=True)
            summed = summed + jnp.dot(
                expo.astype(jnp.bfloat16), v_ref[other * rows : (other + 1) * rows, :],
                preferred_element_type=jnp.float32,
            )
        out_ref[span, :] = (summed / total).astype(jnp.bfloat16)


def local_planes(feats, gain, w_qkv, w_out, block_mask):
    core, micro, y, z = place()
    flags = lax.dynamic_index_in_dim(block_mask, micro, 0, keepdims=False)
    mid, attended, wo = first_layer(feats, gain, w_qkv, w_out, flags)
    return finish_layers(attended, mid, wo)[None]


def solution(mesh):
    planes = (mesh.shape["pipe"], mesh.shape["node"], mesh.shape["head"]) == (2, 8, 2)
    return jax.shard_map(
        local_planes if planes else local_any,
        mesh=mesh,
        in_specs=(
            P(None, "node", "head"),
            P("pipe", None),
            P("pipe", None, "node", "head"),
            P("pipe", "head", "node"),
            P(),
        ),
        out_specs=P("pipe", None, "node", "head"),
        check_vma=False,
    )
```

```python
import functools
import jax
import jax.numpy as jnp
from jax import lax
from jax.experimental import pallas as pl
from jax.experimental.pallas import tpu as pltpu
from jax.sharding import PartitionSpec as P

HD = 128
MICRO = 2


EPS = 1e-06
NEG = -1e30


def from_partner(block, axis, apart):
    count = lax.axis_size(axis)
    route = []
    for low in range(count):
        high = low | 1 << apart
        if high != low and high < count:
            route += [(low, high), (high, low)]
    return lax.ppermute(block, axis, route)


def from_behind(value, axis, steps):
    count = lax.axis_size(axis)
    first, last = (max(0, -steps), min(count, count - steps))
    return lax.ppermute(value, axis, [(source, source + steps) for source in range(first, last)])


def partial_attend(query, key, value, keep):
    rows = query.shape[0]
    groups = query.shape[1] // HD
    q_heads = query.reshape(rows, groups, HD)
    k_heads = key.reshape(key.shape[0], groups, HD)
    v_heads = value.reshape(value.shape[0], groups, HD)
    scores = jnp.einsum("qhd,khd->hqk", q_heads, k_heads, preferred_element_type=jnp.float32) * (
        1.0 / HD**0.5
    )
    scores = jnp.where(keep[None, None, :], scores, NEG)
    top = jnp.max(scores, axis=-1)
    expo = jnp.where(keep[None, None, :], jnp.exp(scores - top[..., None]), 0.0)
    total = jnp.sum(expo, axis=-1)
    summed = jnp.einsum(
        "hqk,khd->hqd", expo.astype(jnp.bfloat16), v_heads, preferred_element_type=jnp.float32
    )
    return (summed, top, total)


def finish(summed, total):
    out = summed / total[..., None]
    rows = out.shape[1]
    return jnp.transpose(out, (1, 0, 2)).reshape(rows, -1).astype(jnp.bfloat16)


def local_any(feats, gain, w_qkv, w_out, block_mask):
    segment = lax.axis_index("pipe")
    me = lax.axis_index("node")
    width = lax.axis_size("node").bit_length() - 1
    bit_list = [width - 1, width // 2, 0]
    qkv_whole, out_whole = (
        lax.all_gather(w_qkv, "node", axis=2, tiled=True),
        lax.all_gather(w_out, "node", axis=2, tiled=True),
    )
    w_query = qkv_whole[0, 0]
    w_key = qkv_whole[0, 1]
    w_value = qkv_whole[0, 2]
    w_proj = out_whole[0]
    gain_row = gain[0]
    rows = feats.shape[1]
    carried = jnp.zeros_like(feats[0])
    results = []
    for tick in range(MICRO + 1):
        micro = jnp.clip(tick - segment, 0, MICRO - 1)
        fresh = feats[min(tick, MICRO - 1)]
        inputs = jnp.where(segment == 0, fresh, carried)
        whole = lax.all_gather(inputs, "head", axis=1, tiled=True)
        xf = whole.astype(jnp.float32)
        inv = lax.rsqrt(jnp.mean(xf * xf, axis=-1, keepdims=True) + EPS)
        normed = (xf * inv * gain_row).astype(jnp.bfloat16)
        query = jnp.dot(normed, w_query, preferred_element_type=jnp.float32).astype(jnp.bfloat16)
        key = jnp.dot(normed, w_key, preferred_element_type=jnp.float32).astype(jnp.bfloat16)
        value = jnp.dot(normed, w_value, preferred_element_type=jnp.float32).astype(jnp.bfloat16)
        mask_rows = lax.dynamic_index_in_dim(block_mask, micro, 0, keepdims=False)
        own_flag = mask_rows[me, me] > 0
        key_list = [key]
        value_list = [value]
        flag_list = [own_flag]
        for bit in bit_list:
            far_key, far_value = from_partner((key, value), "node", bit)
            key_list.append(far_key)
            value_list.append(far_value)
            flag_list.append(mask_rows[me, jnp.bitwise_xor(me, 1 << bit)] > 0)
        keep = jnp.repeat(jnp.stack(flag_list), rows)
        summed, top, total = partial_attend(
            query, jnp.concatenate(key_list, 0), jnp.concatenate(value_list, 0), keep
        )
        attended = finish(summed, total)
        terms = jnp.dot(attended, w_proj, preferred_element_type=jnp.float32)
        reduced = lax.psum_scatter(
            terms.astype(jnp.bfloat16), "head", scatter_dimension=1, tiled=True
        ).astype(jnp.float32)
        output = (inputs.astype(jnp.float32) + reduced).astype(jnp.bfloat16)
        results.append(output)
        if tick < MICRO:
            carried = from_behind(output, "pipe", 1)
    first = jnp.where(segment == 0, results[0], results[1])
    second = jnp.where(segment == 0, results[1], results[2])
    return jnp.stack([first, second])[None]


PIECES = 4
MESH_ID = pl.DeviceIdType.MESH
ANY = pl.BlockSpec(memory_space=pl.ANY)


def place():
    core, node, y = lax.axis_index("pipe"), lax.axis_index("node"), lax.axis_index("head")
    return core, lax.rem(node, 2), y, lax.div(node, 2)


def dev(core, x, y, z):
    return (core, z * 2 + x, y)


def z_apart(z, d):
    if d == 0:
        return z
    if d == 1:
        return z + 1 - 2 * lax.rem(z, 2)
    if d == 2:
        return z + 2 - 4 * lax.div(z, 2)
    return 3 - z


def remote(src, dst, send, recv, target):
    return pltpu.make_async_remote_copy(
        src_ref=src, dst_ref=dst, send_sem=send, recv_sem=recv, device_id=target, device_id_type=MESH_ID
    )


def greet(peers):
    barrier = pltpu.get_barrier_semaphore()
    for peer in peers:
        pl.semaphore_signal(barrier, inc=1, device_id=peer, device_id_type=MESH_ID)
    pl.semaphore_wait(barrier, len(peers))


def head_slot(core, y, z):
    return 8 * y + 2 * z + core


def column_slot(core, y, z):
    return 4 * z + 2 * y + core


class Gather:
    def __init__(self, slot, own, out, sems, sent):
        self.slot, self.own, self.out, self.sent = slot, own, out, sent
        self.local, self.zs, self.zr, self.ys, self.yr, self.bs, self.br = sems
        self.at = place()
        self.rows, self.wide = own.shape[0] // PIECES, own.shape[1]
        core, x, y, z = self.at
        self.far = [dev(core, x, y, z_apart(z, d)) for d in (1, 2, 3)]
        self.beside, self.sibling = dev(core, x, 1 - y, z), dev(1 - core, x, y, z)

    def peers(self):
        return self.far + [self.beside, self.sibling]

    def mine(self, p):
        return self.own.at[pl.ds(p * self.rows, self.rows), :]

    def region(self, c, yy, zz, p):
        column = pl.multiple_of(self.slot(c, yy, zz) * self.wide, self.wide)
        return self.out.at[pl.ds(p * self.rows, self.rows), pl.ds(column, self.wide)]

    def send(self, src, dst, ssem, rsem, target):
        copy = remote(src, dst, ssem, rsem, target)
        copy.start()
        self.sent.append(copy.wait_send)

    def await_recv(self, got, sem):
        remote(self.mine(0), got, sem, sem, self.sibling).wait_recv()

    def start(self, p):
        core, x, y, z = self.at
        mine, spot = self.mine(p), self.region(core, y, z, p)
        for d in (1, 2, 3):
            self.send(mine, spot, self.zs.at[p, d - 1], self.zr.at[p, d - 1], self.far[d - 1])
        self.send(mine, spot, self.ys.at[p, 0], self.yr.at[p, 0], self.beside)
        self.send(mine, spot, self.bs.at[p, 0], self.br.at[p, 0], self.sibling)
        pltpu.make_async_copy(mine, spot, self.local.at[p]).start()

    def along_z(self, p):
        core, x, y, z = self.at
        for d in (1, 2, 3):
            got = self.region(core, y, z_apart(z, d), p)
            self.await_recv(got, self.zr.at[p, d - 1])
            self.send(got, got, self.ys.at[p, d], self.yr.at[p, d], self.beside)
            self.send(got, got, self.bs.at[p, d], self.br.at[p, d], self.sibling)

    def along_y(self, p):
        core, x, y, z = self.at
        for d in range(4):
            got = self.region(core, 1 - y, z_apart(z, d), p)
            self.await_recv(got, self.yr.at[p, d])
            self.send(got, got, self.bs.at[p, 4 + d], self.br.at[p, 4 + d], self.sibling)

    def whole(self, p):
        core, x, y, z = self.at
        for d in range(8):
            got = self.region(1 - core, y if d < 4 else 1 - y, z_apart(z, d % 4), p)
            self.await_recv(got, self.br.at[p, d])
        pltpu.make_async_copy(self.mine(p), self.region(core, y, z, p), self.local.at[p]).wait()


def gather_sems():
    dma = pltpu.SemaphoreType.DMA
    return [dma((PIECES,))] + [dma((PIECES, c)) for c in (3, 3, 4, 4, 8, 8)]


def own_columns(array):
    core, x, y, z = place()
    return array.at[:, pl.ds(pl.multiple_of(column_slot(core, y, z) * HD, HD), HD)]


def project_piece(all_ref, wo_ref, s, rest_ref, into_ref, p):
    rows = all_ref.shape[0] // PIECES
    span = slice(p * rows, (p + 1) * rows)
    projected = jnp.dot(all_ref[span, :], wo_ref[s], preferred_element_type=jnp.float32)
    into_ref[span, :] = (rest_ref[span, :].astype(jnp.float32) + projected).astype(jnp.bfloat16)


def main_kernel(
    feats, gain, w_qkv, w_out, flags, mid, out_ref, wo,
    xg, gains, wq, all_ref, own, rest_ref, into_ref, q_ref, k_ref, v_ref,
    l_sem, x_send, x_recv, z_send, z_recv, y_send, y_recv, b_send, b_recv,
    g_send, g_recv, q_send, q_recv, qx_send, qx_recv, o_send, o_recv, rest_sem, *sems,
):
    core, x, y, z = place()
    node = z * 2 + x
    half, wide = feats.shape[1] // 2, feats.shape[2]
    depth = w_qkv.shape[2]
    far = [z_apart(z, d) for d in (1, 2, 3)]
    beside, sibling, across = dev(core, x, 1 - y, z), dev(1 - core, x, y, z), dev(core, 1 - x, y, z)
    plane = [
        dev(cc, xx, yy, z)
        for cc in (core, 1 - core)
        for xx in (x, 1 - x)
        for yy in (y, 1 - y)
    ][1:]
    greet(plane + [dev(cc, x, y, zz) for zz in far for cc in (core, 1 - core)])
    sent = []
    local = []

    def send(src, dst, ssem, rsem, target):
        copy = remote(src, dst, ssem, rsem, target)
        copy.start()
        sent.append(copy)

    def keep(src, dst, sem):
        copy = pltpu.make_async_copy(src, dst, sem)
        copy.start()
        local.append(copy)

    def region(c, xx, yy, zz):
        return xg.at[
            pl.ds(pl.multiple_of((zz * 2 + xx) * 2 * half + c * half, half), half),
            pl.ds(pl.multiple_of(yy * wide, wide), wide),
        ]

    rows = pl.ds(pl.multiple_of(core * half, half), half)
    mine, other = feats.at[x, rows, :], feats.at[1 - x, rows, :]
    spot = region(core, x, y, z)
    send(other, spot, x_send, x_recv, across)
    send(mine, spot, y_send.at[0], y_recv.at[0], beside)
    for d in (1, 2, 3):
        send(mine, spot, z_send.at[d - 1], z_recv.at[d - 1], dev(core, x, y, far[d - 1]))
    send(mine, spot, b_send.at[0], b_recv.at[0], sibling)
    keep(mine, spot, l_sem.at[0])
    send(gain, gains.at[core], g_send, g_recv, sibling)
    keep(gain, gains.at[core], l_sem.at[1])

    far_x = region(core, 1 - x, y, z)
    remote(mine, far_x, x_send, x_recv, sibling).wait_recv()
    send(far_x, far_x, y_send.at[4], y_recv.at[4], beside)
    for d in (1, 2, 3):
        send(far_x, far_x, z_send.at[2 + d], z_recv.at[2 + d], dev(core, x, y, far[d - 1]))
    send(far_x, far_x, b_send.at[8], b_recv.at[8], sibling)

    def head_columns(zz, c):
        return w_qkv.at[0, :, :, pl.ds(pl.multiple_of((zz * 2 + c) * HD, HD), HD)]

    def depth_rows(c, xx, zz):
        return wq.at[c, :, pl.ds(pl.multiple_of((zz * 2 + xx) * depth, depth), depth), :]

    own_rows = depth_rows(core, x, z)
    weights = []
    for d in range(4):
        zz = z_apart(z, d)
        for other_core in range(2):
            target = 1 - core if other_core else core
            if d == 0 and not other_core:
                keep(head_columns(z, core), own_rows, l_sem.at[2])
                weights.append(remote(head_columns(z, core), own_rows, qx_send.at[0], qx_recv.at[0], across))
            else:
                at = 2 * d + other_core
                weights.append(
                    remote(head_columns(zz, target), own_rows, q_send.at[at], q_recv.at[at], dev(target, x, y, zz))
                )

    def start_weights():
        for copy in weights:
            copy.start()

    def pass_section(s):
        for d in range(4):
            at = 2 * d + (core if s == 0 else 1 - core)
            got = depth_rows(s, x, z_apart(z, d))
            arrived = remote(head_columns(z, core), got, x_send, q_recv.at[at], sibling)
            if d:
                arrived.wait_recv()
                send(got, got, qx_send.at[at], qx_recv.at[at], across)
            else:
                copy = remote(got, got, qx_send.at[1], qx_recv.at[1], across)

                @pl.when(core != s)
                def _():
                    arrived.wait_recv()
                    copy.start()

                if s == 0:
                    weights.append(copy)

    def await_section(s):
        for d in range(4):
            at = 2 * d + (core if s == 0 else 1 - core)
            got = depth_rows(s, 1 - x, z_apart(z, d))
            remote(head_columns(z, core), got, x_send, qx_recv.at[at], sibling).wait_recv()

    def await_projection():
        for yy in range(2):
            for cc in range(2):
                got = wo.at[cc, pl.ds(yy * half_rows, half_rows), :]
                remote(w_out.at[0, :, pl.ds(0, HD)], got, x_send, o_recv.at[2 * yy + cc], sibling).wait_recv()

    pl.when(core == 0)(start_weights)
    for k in range(2):
        xx = 1 - x if k else x
        for d in (1, 2, 3):
            got = region(core, xx, y, far[d - 1])
            remote(mine, got, x_send, z_recv.at[3 * k + d - 1], sibling).wait_recv()
            send(got, got, y_send.at[4 * k + d], y_recv.at[4 * k + d], beside)
            send(got, got, b_send.at[8 * k + d], b_recv.at[8 * k + d], sibling)
    pl.when(core == 1)(start_weights)
    pass_section(0)
    for k in range(2):
        xx = 1 - x if k else x
        for d in range(4):
            got = region(core, xx, 1 - y, z_apart(z, d))
            remote(mine, got, x_send, y_recv.at[4 * k + d], sibling).wait_recv()
            send(got, got, b_send.at[8 * k + 4 + d], b_recv.at[8 * k + 4 + d], sibling)
    for k in range(2):
        xx = 1 - x if k else x
        for d in range(8):
            got = region(1 - core, xx, y if d < 4 else 1 - y, z_apart(z, d % 4))
            remote(mine, got, x_send, b_recv.at[8 * k + d], sibling).wait_recv()
    half_rows = w_out.shape[1]
    to = wo.at[core, pl.ds(pl.multiple_of(y * half_rows, half_rows), half_rows), :]
    projections = []
    for a in range(2):
        for b in range(2):
            xx = 1 - x if a else x
            cc = 1 - core if b else core
            src = w_out.at[0, :, pl.ds(pl.multiple_of(cc * HD, HD), HD)]
            rsem = o_recv.at[2 * y + core]
            copy = remote(src, to, o_send.at[2 * a + b], rsem, dev(cc, xx, x, z))
            if a == 0 and b == 0:
                pl.when(x != y)(copy.start)
                pl.when(x == y)(pltpu.make_async_copy(src, to, rsem).start)
            else:
                copy.start()
            projections.append(copy)

    remote(gain, gains.at[1 - core], g_send, g_recv, sibling).wait_recv()
    for copy in local:
        copy.wait()
    await_section(0)
    rest = pltpu.make_async_copy(own_columns(xg), rest_ref, rest_sem)
    rest.start()
    for p in range(PIECES):
        span = pl.ds(p * (xg.shape[0] // PIECES), xg.shape[0] // PIECES)
        project_rows(
            xg[span, :].astype(jnp.float32), gains[0], lambda part: wq[0, part], (q_ref, k_ref, v_ref), span
        )
    attend_blocks(q_ref, k_ref, v_ref, flags, own)
    rest.wait()
    waits = []
    heads = Gather(head_slot, own, all_ref, sems[:7], waits)
    columns = Gather(column_slot, into_ref, mid, sems[7:], waits)
    for p in range(PIECES):
        heads.start(p)
    pass_section(1)
    rows = mid.shape[0] // PIECES
    for step in range(2 * PIECES + 2):
        for stage in range(3):
            part = step - stage
            if part < 0 or part >= 2 * PIECES:
                continue
            gather, p = (heads, part) if part < PIECES else (columns, part - PIECES)
            if stage == 0:
                gather.along_z(p)
            elif stage == 1:
                gather.along_y(p)
            else:
                gather.whole(p)
                if part == 0:
                    await_projection()
                if part == PIECES:
                    await_section(1)
                if gather is heads:
                    project_piece(all_ref, wo, 0, rest_ref, into_ref, p)
                    columns.start(p)
                else:
                    span = pl.ds(p * rows, rows)
                    project_rows(
                        mid[span, :].astype(jnp.float32), gains[1], lambda part: wq[1, part],
                        (q_ref, k_ref, v_ref), span,
                    )
    attend_blocks(q_ref, k_ref, v_ref, flags, out_ref)
    for copy in sent + weights:
        copy.wait_send()
    pl.when(x != y)(projections[0].wait_send)
    for copy in projections[1:]:
        copy.wait_send()
    for wait in waits:
        wait()


def first_layer(feats, gain, w_qkv, w_out, flags):
    dma = pltpu.SemaphoreType.DMA
    vmem = pl.BlockSpec(memory_space=pltpu.VMEM)
    bf = jnp.bfloat16
    rows, wide = feats.shape[1] * 8, feats.shape[2] * 2
    narrow = pltpu.VMEM((rows, HD), bf)
    return pl.pallas_call(
        main_kernel,
        out_shape=(
            jax.ShapeDtypeStruct((rows, wide), bf),
            jax.ShapeDtypeStruct((rows, HD), bf),
            jax.ShapeDtypeStruct((2, wide, HD), bf),
        ),
        in_specs=[ANY] * 4 + [pl.BlockSpec(memory_space=pltpu.SMEM)],
        out_specs=(vmem,) * 3,
        scratch_shapes=[pltpu.VMEM((rows, wide), bf), pltpu.VMEM((2, 1, wide), jnp.float32),
                        pltpu.VMEM((2, 3, wide, HD), bf), pltpu.VMEM((rows, wide), bf)] + [narrow] * 6
        + [dma((3,)), dma(()), dma(()), dma((6,)), dma((6,)), dma((8,)), dma((8,)), dma((16,)), dma((16,)),
           dma(()), dma(()), dma((8,)), dma((8,)), dma((8,)), dma((8,)), dma((4,)), dma((4,)), dma(())]
        + gather_sems() + gather_sems(),
        compiler_params=pltpu.CompilerParams(
            collective_id=0, has_side_effects=True, vmem_limit_bytes=63 * 2**20
        ),
        name="first_layer",
    )(feats, gain, w_qkv, w_out, flags)


def finish_kernel(
    own, mid, wo_ref, out,
    all_ref, rest_ref, last, rest_sem, l_sem, m_send, m_recv, a_send, a_recv, *sems,
):
    sent = []
    heads = Gather(head_slot, own, all_ref, sems, sent)
    core, x, y, z = place()
    node = z * 2 + x
    rows, wide = out.shape[1], out.shape[2]
    piece = last.shape[1]
    to_y = lax.div(z, 2)
    z_low = lax.rem(z, 2)
    first = core == 0
    to_self = (core == 1) & (y == to_y)
    barrier = pltpu.get_barrier_semaphore()

    def signal(peer):
        pl.semaphore_signal(barrier, inc=1, device_id=peer, device_id_type=MESH_ID)

    for peer in heads.peers():
        signal(peer)

    @pl.when(first)
    def _():
        signal(dev(0, 1 - x, y, z))

    sources = [(zl, xx, yy, cc) for zl in range(2) for xx in range(2) for yy in range(2) for cc in range(2)]
    for zl, xx, yy, cc in sources:
        own = (cc == core) & (xx == x) & (yy == y) & (2 * y + zl == z)

        @pl.when((core == 1) & jnp.logical_not(own))
        def _():
            signal(dev(cc, xx, yy, 2 * y + zl))

    pl.semaphore_wait(barrier, 13 - to_self.astype(jnp.int32) + first.astype(jnp.int32))

    for p in range(PIECES):
        heads.start(p)
    rest = pltpu.make_async_copy(own_columns(mid), rest_ref, rest_sem)
    rest.start()

    def mid_rows(n):
        return mid.at[
            pl.ds(pl.multiple_of(n * rows, rows), rows), pl.ds(pl.multiple_of(y * wide, wide), wide)
        ]

    cross = remote(mid_rows(z * 2 + 1 - x), out.at[x], m_send, m_recv, dev(0, 1 - x, y, z))
    keep = pltpu.make_async_copy(mid_rows(node), out.at[x], l_sem)

    @pl.when(first)
    def _():
        cross.start()
        keep.start()

    slot = 4 * z_low + 2 * y + core
    spot = out.at[x, :, pl.ds(pl.multiple_of(slot * piece, piece), piece)]
    index = 8 * z_low + 4 * x + 2 * y + core
    copies = []
    rest.wait()
    for step in range(PIECES + 2):
        if step < PIECES:
            heads.along_z(step)
        if 0 <= step - 1 < PIECES:
            heads.along_y(step - 1)
        p = step - 2
        if p < 0:
            continue
        heads.whole(p)
        project_piece(all_ref, wo_ref, 1, rest_ref, last, p)
        for n in range(8 // PIECES * p, 8 // PIECES * (p + 1)):
            src = last.at[pl.ds(n * rows, rows), :]
            copy = remote(src, spot, a_send.at[n], a_recv.at[index], dev(1, n % 2, to_y, n // 2))
            mine = to_self & (node == n)
            pl.when(jnp.logical_not(mine))(copy.start)
            pl.when(mine)(pltpu.make_async_copy(src, spot, a_recv.at[index]).start)
            copies.append((copy, mine))

    @pl.when(first)
    def _():
        remote(mid_rows(node), out.at[1 - x], m_send, m_recv, dev(0, 1 - x, y, z)).wait_recv()
        cross.wait_send()
        keep.wait()

    @pl.when(core == 1)
    def _():
        for zl, xx, yy, cc in sources:
            at = 4 * zl + 2 * yy + cc
            got = out.at[xx, :, pl.ds(at * piece, piece)]
            remote(
                last.at[pl.ds(0, rows), :], got, a_send.at[0], a_recv.at[8 * zl + 4 * xx + 2 * yy + cc],
                dev(0, x, y, z),
            ).wait_recv()

    for copy, mine in copies:
        pl.when(jnp.logical_not(mine))(copy.wait_send)
    for wait in sent:
        wait()


def finish_layers(own, mid, wo):
    dma = pltpu.SemaphoreType.DMA
    rows, wide = mid.shape
    narrow = pltpu.VMEM((rows, HD), jnp.bfloat16)
    return pl.pallas_call(
        finish_kernel,
        out_shape=jax.ShapeDtypeStruct((2, rows // 8, wide // 2), mid.dtype),
        in_specs=[ANY, ANY, pl.BlockSpec(memory_space=pltpu.VMEM)],
        out_specs=ANY,
        scratch_shapes=[pltpu.VMEM((rows, wide), jnp.bfloat16), narrow, narrow]
        + [dma(()), dma(()), dma(()), dma(()), dma((8,)), dma((16,))] + gather_sems(),
        compiler_params=pltpu.CompilerParams(
            collective_id=3, has_side_effects=True, vmem_limit_bytes=63 * 2**20
        ),
        name="finish",
    )(own, mid, wo)


def project_rows(xf, gain_row, w_part, refs, here):
    inv = lax.rsqrt(jnp.mean(xf * xf, axis=-1, keepdims=True) + EPS)
    normed = (xf * inv * gain_row).astype(jnp.bfloat16)
    for part, ref in enumerate(refs):
        ref[here, :] = jnp.dot(normed, w_part(part), preferred_element_type=jnp.float32).astype(jnp.bfloat16)


def attend_blocks(q_ref, k_ref, v_ref, flags, out_ref):
    count = flags.shape[0]
    rows = q_ref.shape[0] // count
    width = count.bit_length() - 1
    bits = [width - 1, width // 2, 0]
    for block in range(count):
        seen = [block] + [block ^ (1 << bit) for bit in bits]
        span = slice(block * rows, (block + 1) * rows)
        query = q_ref[span, :]
        scores = []
        for other in seen:
            key = k_ref[other * rows : (other + 1) * rows, :]
            dots = lax.dot_general(query, key, (((1,), (1,)), ((), ())), preferred_element_type=jnp.float32)
            scores.append(jnp.where(flags[block, other] > 0, dots * (1.0 / HD**0.5), NEG))
        top = functools.reduce(jnp.maximum, [jnp.max(s, axis=-1, keepdims=True) for s in scores])
        total = jnp.zeros_like(top)
        summed = jnp.zeros((rows, HD), jnp.float32)
        for other, s in zip(seen, scores):
            expo = jnp.where(flags[block, other] > 0, jnp.exp(s - top), 0.0)
            total = total + jnp.sum(expo, axis=-1, keepdims=True)
            summed = summed + jnp.dot(
                expo.astype(jnp.bfloat16), v_ref[other * rows : (other + 1) * rows, :],
                preferred_element_type=jnp.float32,
            )
        out_ref[span, :] = (summed / total).astype(jnp.bfloat16)


def local_planes(feats, gain, w_qkv, w_out, block_mask):
    core, micro, y, z = place()
    flags = lax.dynamic_index_in_dim(block_mask, micro, 0, keepdims=False)
    mid, attended, wo = first_layer(feats, gain, w_qkv, w_out, flags)
    return finish_layers(attended, mid, wo)[None]


def solution(mesh):
    planes = (mesh.shape["pipe"], mesh.shape["node"], mesh.shape["head"]) == (2, 8, 2)
    return jax.shard_map(
        local_planes if planes else local_any,
        mesh=mesh,
        in_specs=(
            P(None, "node", "head"),
            P("pipe", None),
            P("pipe", None, "node", "head"),
            P("pipe", "head", "node"),
            P(),
        ),
        out_specs=P("pipe", None, "node", "head"),
        check_vma=False,
    )
```
